128 devices in a mesh: blk: 2 (over x_lo), mblk: 64 (over z, y, x_hi, core).
Axes of the slice: x: 4 (x_hi: 2, x_lo: 2; x = x_hi * 2 + x_lo), y: 4, z: 4, core: 2. Of those that a mesh axis runs over, the one named last changes fastest.
Arguments:
- pixels: float32 [2048, 1024], P(('blk', 'mblk')), may hold values from -6 to 6
- block_ids: int32 [2048], P(('blk', 'mblk')), may hold values from 0 to 2047, as said below
- block_mask: int32 [2048], P(('blk', 'mblk')), may hold values 0 or 1
- model_cl: float32 [4096], replicated, may hold values from 0.5 to 1.5
Outputs:
- pseudo_cl: float32 [4096], replicated
- misfit: float32 [], replicated
The draws below stay inside these ranges and needn't reach their ends.
Inputs may be any that keep to these rules, and one draw needn't show every extreme that they name: block_ids holds every block number once. The device at blk index s and mblk index j holds, for every blk index b, exactly 8 blocks of the cycles of the device at blk index b and mblk index j, where cycle r belongs to the device at blk index r // 128 and mblk index (r % 128) // 2.
All inputs are finite; a program needn't handle non-finite values. No bound on the sum of `block_mask` on one device may be relied on, other than what follows from the above.
Results may differ from the reference program's by a relative error of at most 0.0003.
Values sent between devices are 32-bit elements; how exact they have to be, the bound alone decides.
A program may use at most 64 MiB of HBM per device.

```python
import math
import jax
import jax.numpy as jnp
from jax import lax

NSIDE = 2048
CYCLE_PIX = 8192
LMAX = 4096
BLOCK_PIX = 1024
CYCLES = 256
SLOTS = 16
CAP = 8
BLOCKS = 2048
N_BLK = 2
N_MBLK = 64


def draw_block_ids(key, part):
    owner_key, slot_key = jax.random.split(key)
    owner_total = N_BLK * N_MBLK
    owner_perm = jax.vmap(lambda sub_key: jax.random.permutation(sub_key, SLOTS))(jax.random.split(owner_key, owner_total))
    slot_perm = jax.vmap(lambda sub_key: jax.random.permutation(sub_key, SLOTS))(jax.random.split(slot_key, owner_total))
    source = jnp.arange(N_BLK, dtype=jnp.int32)[:, None, None]
    column = jnp.arange(N_MBLK, dtype=jnp.int32)[None, :, None]
    initial = slot_perm.reshape(N_BLK, N_MBLK, SLOTS).astype(jnp.int32)
    band_idx = initial // CAP
    within = initial % CAP
    owner = band_idx * N_MBLK + column
    picked = owner_perm.astype(jnp.int32)[owner, source * CAP + within]
    return (owner * SLOTS + picked).reshape(-1).astype(jnp.int32)


def plant(entries, key, smallest, top_value):
    shape = entries.shape
    place = [jax.random.randint(jax.random.fold_in(key, axis), (), 0, shape[axis]) for axis in range(len(shape))]
    entries = entries.at[tuple(place)].set(smallest)
    longest = shape.index(max(shape))
    place[longest] = (place[longest] + 1) % shape[longest]
    return entries.at[tuple(place)].set(top_value)


def levels(key, dims, pieces, low, largest):
    def one(position, parts):
        steps = jax.random.uniform(jax.random.fold_in(jax.random.fold_in(key, 6), position), (parts,), jnp.float32, low / len(pieces), largest / len(pieces))
        return jnp.repeat(jnp.exp(steps), dims[position] // parts).reshape((-1,) + (1,) * (len(dims) - position - 1))

    loudness = one(*pieces[0])
    for cut in pieces[1:]:
        loudness = loudness * one(*cut)
    return loudness


def scatter_about(rng, shape, scale, limit, cuts=(), kind=jnp.bfloat16):
    array = scale * jax.random.normal(rng, shape, jnp.float32)
    if cuts:
        array = array * levels(rng, shape, cuts, -0.22, 0.18)
    return jnp.clip(array, -limit, limit).astype(kind)


def setup_inputs(seed: int = 0) -> dict:
    keys = jax.random.split(jax.random.key(seed), 5)
    pixels = scatter_about(keys[0], (BLOCKS, BLOCK_PIX), 1.0, 6.0, ((0, 128),), jnp.float32)
    block_ids = draw_block_ids(jax.random.fold_in(keys[4], 71), 0)
    block_mask = plant((jax.random.randint(keys[2], (BLOCKS,), 0, 4) < 3).astype(jnp.int32), jax.random.fold_in(keys[2], 1), 0, 1)
    model_cl = jnp.clip(jax.random.uniform(keys[3], (LMAX,), jnp.float32, 0.5, 1.5), 0.5, 1.5)
    return {"pixels": pixels, "block_ids": block_ids, "block_mask": block_mask, "model_cl": model_cl}


def log_products(degree_count):
    counter = jnp.arange(1, degree_count, dtype=jnp.int32).astype(jnp.float32)
    return jnp.concatenate([jnp.zeros((1,), jnp.float32), jnp.cumsum(jnp.log1p(-0.5 / counter))])

def seeds_for(latitude, orders_f, log_prod):
    base_log = 0.5 * (jnp.log(2.0 * orders_f + 1.0) - math.log(4.0 * math.pi)) + 0.5 * log_prod
    return jnp.exp(base_log[None, :] + 0.5 * orders_f[None, :] * jnp.log1p(-latitude[:, None] * latitude[:, None]))

def coefficients(degree_f, orders_f):
    alpha_term = jnp.sqrt((2.0 * degree_f - 1.0) * (2.0 * degree_f + 1.0) / jnp.maximum((degree_f - orders_f) * (degree_f + orders_f), 1.0))
    beta_term = alpha_term * jnp.sqrt(jnp.maximum((degree_f - 1.0 - orders_f) * (degree_f - 1.0 + orders_f), 0.0) / jnp.maximum((2.0 * degree_f - 3.0) * (2.0 * degree_f - 1.0), 1.0))
    return (alpha_term, beta_term)

def advance(degree, orders, latitude, prev_one, prev_two, seed_vals):
    degree_f = degree.astype(jnp.float32)
    orders_f = orders.astype(jnp.float32)
    alpha_term, beta_term = coefficients(degree_f, orders_f)
    grown = alpha_term[None, :] * latitude[:, None] * prev_one - beta_term[None, :] * prev_two
    return jnp.where(degree > orders[None, :], grown, jnp.where(degree == orders[None, :], seed_vals, 0.0))

def reference(pixels, block_ids, block_mask, model_cl):
    kept = pixels * block_mask[:, None].astype(jnp.float32)
    cycle_map = jnp.zeros_like(kept).at[block_ids].set(kept).reshape(CYCLES, CYCLE_PIX)
    cycle_idx = jnp.arange(CYCLES, dtype=jnp.int32)
    latitude = (CYCLES // 2 - cycle_idx).astype(jnp.float32) * (2.0 / (3.0 * NSIDE))
    half_shift = jnp.where(cycle_idx % 2 == 0, 0.5, 0.0).astype(jnp.float32)
    full_fft = jnp.fft.rfft(cycle_map, axis=1)[:, :LMAX]
    raw_re = jnp.real(full_fft)
    raw_im = jnp.imag(full_fft)
    orders = jnp.arange(LMAX, dtype=jnp.int32)
    orders_f = orders.astype(jnp.float32)
    phase_angle = half_shift[:, None] * orders_f[None, :] * (2.0 * math.pi / CYCLE_PIX)
    phase_cos = jnp.cos(phase_angle)
    phase_sin = jnp.sin(phase_angle)
    spec_re = raw_re * phase_cos + raw_im * phase_sin
    spec_im = raw_im * phase_cos - raw_re * phase_sin
    seed_vals = seeds_for(latitude, orders_f, log_products(LMAX))
    norm_scale = math.sqrt(4.0 * math.pi / (CYCLES * CYCLE_PIX))

    def advance_row(carried, degree):
        prev_one, prev_two = carried
        fresh_row = advance(degree, orders, latitude, prev_one, prev_two, seed_vals)
        row_re = lax.optimization_barrier(jnp.sum(fresh_row * spec_re, axis=0)) * norm_scale
        row_im = lax.optimization_barrier(jnp.sum(fresh_row * spec_im, axis=0)) * norm_scale
        return ((fresh_row, prev_one), (row_re, row_im))
    zero_state = jnp.zeros((CYCLES, LMAX), jnp.float32)
    _, (alm_re, alm_im) = lax.scan(advance_row, (zero_state, zero_state), orders)
    weights = jnp.where(orders == 0, 1.0, 2.0).astype(jnp.float32)
    power_sum = lax.optimization_barrier(jnp.sum(weights[None, :] * (alm_re * alm_re + alm_im * alm_im), axis=1))
    pseudo_cl = power_sum / (2.0 * orders_f + 1.0)
    rel_error = (pseudo_cl - model_cl) / model_cl
    misfit = jnp.mean(rel_error * rel_error)
    return (pseudo_cl, misfit)
```

```python
import functools
import math

import jax
import jax.numpy as jnp
import numpy as np
from jax import lax
from jax.experimental import pallas as pl
from jax.experimental.pallas import tpu as pltpu
from jax.sharding import PartitionSpec as P

NSIDE = 2048
CYCLE_PIX = 8192
LMAX = 4096
BLOCK_PIX = 1024
CYCLES = 256
DEVICES = 128
MESH = pl.DeviceIdType.MESH
HIGHEST = lax.Precision.HIGHEST
F32 = jnp.float32


def dft_tables():
    k1 = np.arange(64)
    part, seg = np.meshgrid(np.arange(8), np.arange(8), indexing="ij")
    outer = (8 * seg + part).reshape(-1)
    angle = 2.0 * np.pi * ((k1[:, None] * outer[None, :]) % 64) / 64
    stage_one = np.concatenate([np.cos(angle), -np.sin(angle)], axis=0)
    inner = np.arange(128)
    twists = []
    stage_two = []
    upper = np.concatenate([np.arange(32), 63 - np.arange(32)])
    for cycle in range(2):
        shift = 0.5 if cycle == 0 else 0.0
        turn = 2.0 * np.pi * (k1[:, None] * (inner[None, :] + shift)) / CYCLE_PIX
        twists.append(np.stack([np.cos(turn), np.sin(turn)]))
        turn = 2.0 * np.pi * (upper[:, None] * inner[None, :] % 128) / 128 + (
            2.0 * np.pi * upper[:, None] * shift / 128
        )
        cos_two, sin_two = np.cos(turn), np.sin(turn)
        stage_two.append(
            np.concatenate(
                [
                    np.concatenate([cos_two, sin_two], axis=1),
                    np.concatenate([-sin_two, cos_two], axis=1),
                ],
                axis=0,
            )
        )
    return (
        stage_one.astype(np.float32),
        np.stack(twists).astype(np.float32),
        np.stack(stage_two).astype(np.float32),
    )


def half_logs():
    lat = (CYCLES // 2 - np.arange(CYCLES)) * (2.0 / (3.0 * NSIDE))
    return (0.5 * np.log1p(-lat * lat)).astype(np.float32)


def ratio_table():
    steps = np.arange(1, 4200, dtype=np.float64)
    prods = np.concatenate([[1.0], np.cumprod((2.0 * steps - 1.0) / (2.0 * steps))])
    j = np.arange(8384)
    even = 1.0 / (np.maximum(j, 1) * prods[j // 2])
    odd = prods[np.maximum(j - 1, 0) // 2]
    f = np.where(j % 2 == 0, even, odd)
    f[0] = 1.0
    return f


def degree_tables():
    f = ratio_table()
    step, lane = np.arange(128) // 16, np.arange(128) % 16
    diff = 8 * np.arange(528)[:, None] + (step - lane)[None, :]
    low = np.where(diff >= 0, f[np.maximum(diff, 0)], 0.0)
    high = f[8 * np.arange(1040)[:, None] + (step + lane)[None, :]]
    return low.astype(np.float32), high.astype(np.float32)


def fold_matrix():
    out = np.zeros((2, 2, 64, 128))
    for u in range(64):
        for c in range(2):
            south = 65 + u if c == 0 else 64 + u
            for odd in range(2):
                out[odd, c, u, 63 - u] += 1.0
                if south < 128:
                    out[odd, c, u, south] += -1.0 if odd else 1.0
    arrival = np.arange(128)
    y_source, x_source = arrival // 8, arrival % 8
    owner = (x_source // 4) * 64 + y_source * 4 + x_source % 4
    return out.reshape(256, 128)[:, owner].astype(np.float32)


EQUATOR_ROW = 4


def fourier_body(owner, own_ref, own_ids_ref, own_mask_ref, got_ref, got_ids_ref, got_mask_ref, one_ref, twist_ref, two_ref, logs_ref, out_ref):
    slot = lax.broadcasted_iota(jnp.int32, (16, 16), 0) + owner * 16
    pick_own = jnp.where(own_ids_ref[...] == slot, own_mask_ref[...], 0).astype(F32)
    pick_got = jnp.where(got_ids_ref[...] == slot, got_mask_ref[...], 0).astype(F32)
    rows = jnp.dot(pick_own, own_ref[...], precision=HIGHEST, preferred_element_type=F32) + jnp.dot(
        pick_got, got_ref[...], precision=HIGHEST, preferred_element_type=F32
    )
    folded = jnp.concatenate(
        [
            jnp.concatenate([rows[8 * c : 8 * c + 8, 128 * p : 128 * p + 128] for p in range(8)], axis=0)
            for c in range(2)
        ],
        axis=1,
    )
    first = jnp.dot(one_ref[...], folded, precision=HIGHEST, preferred_element_type=F32)
    k1 = lax.broadcasted_iota(jnp.int32, (64, 64), 1)
    row = lax.broadcasted_iota(jnp.int32, (64, 64), 0)
    orders = (k1 + 64 * jnp.where(row < 32, row, 95 - row)).astype(F32)
    outs = []
    for c in range(2):
        re, im = first[0:64, 128 * c : 128 * c + 128], first[64:128, 128 * c : 128 * c + 128]
        cos, sin = twist_ref[c, 0], twist_ref[c, 1]
        turned = jnp.concatenate([re * cos + im * sin, im * cos - re * sin], axis=1)
        spec = lax.dot_general(
            two_ref[c], turned, (((1,), (1,)), ((), ())), precision=HIGHEST, preferred_element_type=F32
        )
        seed = jnp.exp(orders * logs_ref[owner * 2 + c])
        outs.append((spec[0:64] * seed, spec[64:128] * seed))
    for j in range(4):
        pieces = []
        for ri in range(2):
            for half in range(2):
                jj = j if half == 0 else 3 - j
                for c in range(2):
                    pieces.append(outs[c][ri][32 * half : 32 * half + 32, 16 * jj : 16 * jj + 16])
        out_ref[2 * j : 2 * j + 2] = jnp.concatenate(pieces, axis=1).reshape(2, 16, 128)


def tables_body(d, low_ref, high_ref, coef_ref, gain_ref):
    row = lax.broadcasted_iota(jnp.int32, (8, 128), 0)
    lane = lax.broadcasted_iota(jnp.int32, (8, 128), 1)
    order = lane % 16
    offset = 8 * row + lane // 16
    picks = [order + 16 * step for step in range(8)]
    for half in range(2):
        first = 16 * d if half == 0 else 4080 - 16 * d
        start = 0 if half == 0 else 512 - 2 * d
        count = (4096 - first + 63) // 64

        def one(k, carry):
            low = low_ref[pl.ds(pl.multiple_of(8 * k, 8), 8), :]
            high = high_ref[pl.ds(first // 4 + 8 * k, 8), :]
            both = low * high
            t = offset + 64 * k
            degree = t + first
            down = t - order
            up = (degree + first + order).astype(F32)
            coef = both * (2 * degree - 1).astype(F32)
            weight = jnp.where(first + order == 0, 1.0, 2.0) * (1.0 / (CYCLES * CYCLE_PIX))
            denom = jnp.maximum(down.astype(F32), 1.0) * jnp.maximum(up, 1.0) * both
            gain = jnp.where(down >= 0, weight / jnp.where(down >= 0, denom, 1.0), 0.0)
            at = start + 8 * k
            for step in range(8):
                coef_ref[step, pl.ds(at, 8), :] = jnp.take_along_axis(
                    coef, picks[step], axis=1, mode="promise_in_bounds"
                )
                gain_ref[half, pl.ds(first + 64 * k + step, 8, stride=8), :] = jnp.take_along_axis(
                    gain, picks[step], axis=1, mode="promise_in_bounds"
                )
            return carry

        lax.fori_loop(0, count, one, 0)


def prepare(got_ref, fold_ref, state_ref):
    row = lax.broadcasted_iota(jnp.int32, (64, 128), 0)
    lane = lax.broadcasted_iota(jnp.int32, (64, 128), 1)
    folded = jnp.dot(fold_ref[...], got_ref[...], precision=HIGHEST, preferred_element_type=F32)
    is_c0 = (lane % 32) < 16
    even = jnp.where(is_c0, folded[0:64], folded[64:128])
    odd = jnp.where(is_c0, folded[128:192], folded[192:256])
    same = (lane % 2) == 0
    by_parity = (jnp.where(same, even, odd), jnp.where(same, odd, even))
    group = lax.broadcasted_iota(jnp.int32, (8, 128), 1) // 32
    for half in range(2):
        for p in range(2):
            for ri in range(2):
                source = 2 * ri + half
                for v in range(2):
                    total = None
                    for h in range(4):
                        piece = by_parity[p][32 * v + 8 * h : 32 * v + 8 * h + 8]
                        moved = pltpu.roll(piece, (32 * (h - source)) % 128, 1)
                        total = moved if total is None else jnp.where(group == h, moved, total)
                    state_ref[half, 4 * p + 2 * ri + v] = total
    step = lax.broadcasted_iota(jnp.int32, (8, 128), 0)
    lane8 = lax.broadcasted_iota(jnp.int32, (8, 128), 1)
    turn = (step - lane8 % 16) & 3
    sign = jnp.where(turn == 0, 1.0, jnp.where(turn == 2, -1.0, 0.0))
    line = jnp.broadcast_to(got_ref[EQUATOR_ROW : EQUATOR_ROW + 1, :], (8, 128))
    for half in range(2):
        for ri in range(2):
            source = 2 * ri + half
            base = jnp.where(lane8 // 16 == 2 * source, line, 0.0)
            base = base + pltpu.roll(base, 64, 1)
            base = base + pltpu.roll(base, 32, 1)
            base = base + pltpu.roll(base, 16, 1)
            state_ref[half, 8 + ri] = base * sign


def first_order(d, half):
    return 16 * d if half == 0 else 4080 - 16 * d


UNROLL = 8


def legendre_body(d, coef_ref, state_ref, raw_ref):
    row = lax.broadcasted_iota(jnp.int32, (8, 128), 0)
    lane = lax.broadcasted_iota(jnp.int32, (8, 128), 1)
    order = lane % 16
    masks = ((row & 1) == 0, (row & 2) == 0, (row & 4) == 0)
    lats = []
    for v in range(2):
        u = 32 * v + 8 * (lane // 32) + row
        q = 2 * u + jnp.where((lane % 32) < 16, 2, 1)
        lats.append(q.astype(F32) * (2.0 / (3.0 * NSIDE)))

    def merge(level, first, second):
        mask = masks[level]
        shift = 8 - (1 << level)
        return jnp.where(mask, first, second) + pltpu.roll(jnp.where(mask, second, first), shift, 0)

    def eight(half, base, lead, weights, state, seeded, k):
        a0, a1, b0, b1 = state
        stack = {}
        for step in range(8):
            coef = jnp.broadcast_to(coef_ref[step, pl.ds(base + k, 1), :], (8, 128))
            n0 = (coef * lats[0]) * a0 - b0
            n1 = (coef * lats[1]) * a1 - b1
            if seeded is not None:
                start = order == (seeded * 8 + step)
                n0 = jnp.where(start, 1.0, n0)
                n1 = jnp.where(start, 1.0, n1)
            a0, a1, b0, b1 = n0, n1, a0, a1
            p = step % 2
            for ri in range(2):
                term = n0 * weights[4 * p + 2 * ri] + n1 * weights[4 * p + 2 * ri + 1]
                level, idx = 0, step
                while idx % 2 == 1:
                    term = merge(level, stack.pop((ri, level)), term)
                    level, idx = level + 1, idx // 2
                stack[(ri, level)] = term
        for ri in range(2):
            raw_ref[half, ri, lead + k] = stack[(ri, 3)]
        return (a0, a1, b0, b1)

    for half in range(2):
        first = first_order(d, half)
        base = 0 if half == 0 else 512 - 2 * d
        lead = first // 8
        weights = [state_ref[half, n] for n in range(8)]
        zero = jnp.zeros((8, 128), F32)
        for ri in range(2):
            raw_ref[half, ri, pl.ds(first // 128 * 16, 16)] = jnp.zeros((16, 8, 128), F32)
        state = (zero, zero, zero, zero)
        for k in range(2):
            state = eight(half, base, lead, weights, state, k, k)
        def many(n, state):
            for k in range(UNROLL):
                state = eight(half, base, lead, weights, state, None, UNROLL * n + k + 2)
            return state

        lax.fori_loop(0, ((4096 - first) // 8 - 2 + UNROLL - 1) // UNROLL, many, state)


def clear_gain(d, gain_ref):
    for half in range(2):
        tile = pl.multiple_of(first_order(d, half) // 128 * 128, 128)
        gain_ref[half, pl.ds(tile, 128), :] = jnp.zeros((128, 128), F32)


def power_body(d, raw_ref, gain_ref, state_ref, power_ref):
    ones = jnp.full((8, 128), 0.125, F32)
    power_ref[...] = jnp.zeros_like(power_ref)
    for half in range(2):
        equator = [jnp.concatenate([state_ref[half, 8 + ri]] * 16, axis=0) for ri in range(2)]

        def one(tile, carry):
            total = None
            for ri in range(2):
                value = raw_ref[half, ri, pl.ds(16 * tile, 16)].reshape(128, 128)
                for shift in (64, 32, 16):
                    value = value + pltpu.roll(value, shift, 1)
                value = value + equator[ri]
                total = value * value if total is None else total + value * value
            total = total * gain_ref[half, pl.ds(pl.multiple_of(128 * tile, 128), 128), :]
            power_ref[tile] = power_ref[tile] + lax.dot_general(
                ones, total, (((1,), (1,)), ((), ())), precision=HIGHEST, preferred_element_type=F32
            )
            return carry

        lax.fori_loop(first_order(d, half) // 128, 32, one, 0)


def position():
    blk, mblk = lax.axis_index("blk"), lax.axis_index("mblk")
    return blk * 4 + mblk % 4, mblk // 4


def device_at(x, y):
    return (x // 4, y * 4 + x % 4)


def order_block(rank):
    return 4 * (rank % 32) + rank // 32


def greet(x, y):
    barrier = pltpu.get_barrier_semaphore()
    for step in range(1, 8):
        pl.semaphore_signal(barrier, inc=1, device_id=device_at((x + step) % 8, y), device_id_type=MESH)
    for step in range(1, 16):
        pl.semaphore_signal(barrier, inc=1, device_id=device_at(x, (y + step) % 16), device_id_type=MESH)
    pl.semaphore_wait(barrier, 22)


def send(source, target, send_sem, recv_sem, device):
    copy = pltpu.make_async_remote_copy(
        src_ref=source, dst_ref=target, send_sem=send_sem, recv_sem=recv_sem, device_id=device, device_id_type=MESH
    )
    copy.start()
    return copy


def drain(ref, sem):
    pltpu.make_async_copy(ref, ref, sem).wait()


def fourier_kernel(
    own_ref, own_ids_ref, own_mask_ref, one_ref, twist_ref, two_ref, logs_ref, out_ref,
    got_ref, got_ids_ref, got_mask_ref, rows_ref, mid_ref, again_ref, land_ref, pair_send, pair_recv, send_sem, recv_sem,
):
    x, y = position()
    greet(x, y)
    partner = device_at((x + 4) % 8, y)
    pair = [
        send(source, target, pair_send.at[n], pair_recv.at[n], partner)
        for n, (source, target) in enumerate(
            ((own_ref, got_ref), (own_ids_ref, got_ids_ref), (own_mask_ref, got_mask_ref))
        )
    ]
    for copy in pair:
        copy.wait()
    owner = (x // 4) * 64 + y * 4 + x % 4
    fourier_body(
        owner, own_ref, own_ids_ref, own_mask_ref, got_ref, got_ids_ref, got_mask_ref,
        one_ref, twist_ref, two_ref, logs_ref, rows_ref,
    )
    for step in range(1, 8):
        to = (x + step) % 8
        send(rows_ref.at[to], mid_ref.at[x], send_sem.at[0], recv_sem.at[0], device_at(to, y))
    mid_ref[x] = rows_ref[x]
    drain(mid_ref.at[pl.ds(0, 7)], recv_sem.at[0])
    every = mid_ref[...]
    for to in range(16):
        again_ref[to] = jnp.concatenate([every[n, to : to + 1, :] for n in range(8)], axis=0)
    for step in range(1, 16):
        to = (y + step) % 16
        send(again_ref.at[to], land_ref.at[y], send_sem.at[1], recv_sem.at[1], device_at(x, to))
    land_ref[y] = again_ref[y]
    drain(land_ref.at[pl.ds(0, 15)], recv_sem.at[1])
    out_ref[...] = land_ref[...].reshape(128, 128)
    drain(mid_ref.at[pl.ds(0, 7)], send_sem.at[0])
    drain(land_ref.at[pl.ds(0, 15)], send_sem.at[1])


def reduce_kernel(power_ref, model_ref, pseudo_ref, misfit_ref, part_ref, first_ref, second_ref, third_ref, send_sem, recv_sem):
    x, y = position()
    greet(x, y)
    part_ref[...] = jnp.zeros_like(part_ref)
    for n in range(8):
        part_ref[n, 0:4, :] = power_ref[4 * n : 4 * n + 4, :]
    for step in range(1, 8):
        to = (x + step) % 8
        send(part_ref.at[to], first_ref.at[x], send_sem.at[0], recv_sem.at[0], device_at(to, y))
    first_ref[x] = part_ref[x]
    drain(first_ref.at[pl.ds(0, 7)], recv_sem.at[0])
    second_ref[y] = jnp.sum(first_ref[...], axis=0)
    for step in range(1, 16):
        to = (y + step) % 16
        send(second_ref.at[y], second_ref.at[y], send_sem.at[1], recv_sem.at[1], device_at(x, to))
    drain(second_ref.at[pl.ds(0, 15)], recv_sem.at[1])
    third_ref[x] = jnp.sum(second_ref[...], axis=0)
    for step in range(1, 8):
        to = (x + step) % 8
        send(third_ref.at[x], third_ref.at[x], send_sem.at[2], recv_sem.at[2], device_at(to, y))
    drain(third_ref.at[pl.ds(0, 7)], recv_sem.at[2])
    total = jnp.zeros((1, 1), F32)
    for n in range(8):
        pseudo = third_ref[n, 0:4, :]
        model = model_ref[4 * n : 4 * n + 4, :]
        pseudo_ref[4 * n : 4 * n + 4, :] = pseudo
        rel_error = (pseudo - model) / model
        total = total + jnp.sum(rel_error * rel_error, keepdims=True)
    misfit_ref[...] = total * (1.0 / LMAX)
    drain(first_ref.at[pl.ds(0, 7)], send_sem.at[0])
    drain(second_ref.at[pl.ds(0, 15)], send_sem.at[1])
    drain(third_ref.at[pl.ds(0, 7)], send_sem.at[2])


def legendre_kernel(got_ref, fold_ref, low_ref, high_ref, out_ref, coef_ref, gain_ref, state_ref, raw_ref, power_ref):
    x, y = position()
    d = order_block(x * 16 + y)
    clear_gain(d, gain_ref)
    tables_body(d, low_ref, high_ref, coef_ref, gain_ref)
    prepare(got_ref, fold_ref, state_ref)
    legendre_body(d, coef_ref, state_ref, raw_ref)
    power_body(d, raw_ref, gain_ref, state_ref, power_ref)
    out_ref[...] = power_ref[:, 0, :]


LEGENDRE_SCRATCH = lambda: [
    pltpu.VMEM((8, 544, 128), F32),
    pltpu.VMEM((2, 4096 + 64, 128), F32),
    pltpu.VMEM((2, 10, 8, 128), F32),
    pltpu.VMEM((2, 2, 512 + 16, 8, 128), F32),
    pltpu.VMEM((32, 8, 128), F32),
]
VM = pl.BlockSpec(memory_space=pltpu.VMEM)
SM = pl.BlockSpec(memory_space=pltpu.SMEM)


def on_device(pixels, block_ids, block_mask, model_cl):
    one, twist, two = dft_tables()
    dma = pltpu.SemaphoreType.DMA
    received = pl.pallas_call(
        fourier_kernel,
        out_shape=jax.ShapeDtypeStruct((DEVICES, 128), F32),
        in_specs=[VM] * 6 + [SM],
        out_specs=VM,
        scratch_shapes=[
            pltpu.VMEM((16, BLOCK_PIX), F32),
            pltpu.VMEM((1, 16), jnp.int32),
            pltpu.VMEM((1, 16), jnp.int32),
            pltpu.VMEM((8, 16, 128), F32),
            pltpu.VMEM((8, 16, 128), F32),
            pltpu.VMEM((16, 8, 128), F32),
            pltpu.VMEM((16, 8, 128), F32),
            dma((3,)),
            dma((3,)),
            dma((2,)),
            dma((2,)),
        ],
        compiler_params=pltpu.CompilerParams(collective_id=0, has_side_effects=True),
    )(pixels, block_ids.reshape(1, 16), block_mask.reshape(1, 16), one, twist, two, half_logs())
    low, high = degree_tables()
    power = pl.pallas_call(
        legendre_kernel,
        out_shape=jax.ShapeDtypeStruct((32, 128), F32),
        in_specs=[VM] * 4,
        out_specs=VM,
        scratch_shapes=LEGENDRE_SCRATCH(),
        compiler_params=pltpu.CompilerParams(vmem_limit_bytes=40 * 1024 * 1024),
    )(received, fold_matrix(), low, high)
    pseudo_cl, misfit = pl.pallas_call(
        reduce_kernel,
        out_shape=(jax.ShapeDtypeStruct((32, 128), F32), jax.ShapeDtypeStruct((1, 1), F32)),
        in_specs=[VM] * 2,
        out_specs=(VM, VM),
        scratch_shapes=[
            pltpu.VMEM((8, 8, 128), F32),
            pltpu.VMEM((8, 8, 128), F32),
            pltpu.VMEM((16, 8, 128), F32),
            pltpu.VMEM((8, 8, 128), F32),
            dma((3,)),
            dma((3,)),
        ],
        compiler_params=pltpu.CompilerParams(collective_id=1, has_side_effects=True),
    )(power, model_cl.reshape(32, 128))
    return pseudo_cl.reshape(LMAX), misfit.reshape(())


def solution(mesh):
    in_specs = (P(("blk", "mblk"), None), P(("blk", "mblk")), P(("blk", "mblk")), P())
    return jax.shard_map(on_device, mesh=mesh, in_specs=in_specs, out_specs=(P(), P()), check_vma=False)
```

```python
import functools
import math

import jax
import jax.numpy as jnp
import numpy as np
from jax import lax
from jax.experimental import pallas as pl
from jax.experimental.pallas import tpu as pltpu
from jax.sharding import PartitionSpec as P

NSIDE = 2048
CYCLE_PIX = 8192
LMAX = 4096
BLOCK_PIX = 1024
CYCLES = 256
DEVICES = 128
MESH = pl.DeviceIdType.MESH
HIGHEST = lax.Precision.HIGHEST
F32 = jnp.float32
BF16 = jnp.bfloat16
ROWS = 544
TILES = 33
POWER_UNROLL = 3


def dft_tables():
    k1 = np.arange(64)
    part, seg = np.meshgrid(np.arange(8), np.arange(8), indexing="ij")
    outer = (8 * seg + part).reshape(-1)
    angle = 2.0 * np.pi * ((k1[:, None] * outer[None, :]) % 64) / 64
    stage_one = np.concatenate([np.cos(angle), -np.sin(angle)], axis=0)
    inner = np.arange(128)
    twists = []
    stage_two = []
    upper = np.concatenate([np.arange(32), 63 - np.arange(32)])
    for cycle in range(2):
        shift = 0.5 if cycle == 0 else 0.0
        turn = 2.0 * np.pi * (k1[:, None] * (inner[None, :] + shift)) / CYCLE_PIX
        twists.append(np.stack([np.cos(turn), np.sin(turn)]))
        turn = 2.0 * np.pi * (upper[:, None] * inner[None, :] % 128) / 128 + (
            2.0 * np.pi * upper[:, None] * shift / 128
        )
        cos_two, sin_two = np.cos(turn), np.sin(turn)
        stage_two.append(
            np.concatenate(
                [
                    np.concatenate([cos_two, sin_two], axis=1),
                    np.concatenate([-sin_two, cos_two], axis=1),
                ],
                axis=0,
            )
        )
    return (
        stage_one.astype(np.float32),
        np.stack(twists).astype(np.float32),
        np.stack(stage_two).astype(np.float32),
    )


def half_logs():
    lat = (CYCLES // 2 - np.arange(CYCLES)) * (2.0 / (3.0 * NSIDE))
    return (0.5 * np.log1p(-lat * lat)).astype(np.float32)


def ratio_table():
    steps = np.arange(1, 4200, dtype=np.float64)
    prods = np.concatenate([[1.0], np.cumprod((2.0 * steps - 1.0) / (2.0 * steps))])
    j = np.arange(8384)
    even = 1.0 / (np.maximum(j, 1) * prods[j // 2])
    odd = prods[np.maximum(j - 1, 0) // 2]
    f = np.where(j % 2 == 0, even, odd)
    f[0] = 1.0
    return f


def degree_tables():
    f = ratio_table()
    step, lane = np.arange(128) // 16, np.arange(128) % 16
    diff = 8 * np.arange(528)[:, None] + (step - lane)[None, :]
    low = np.where(diff >= 0, f[np.maximum(diff, 0)], 0.0)
    high = f[8 * np.arange(1040)[:, None] + (step + lane)[None, :]]
    return low.astype(np.float32), high.astype(np.float32)


def fold_matrix():
    out = np.zeros((2, 2, 64, 128))
    for u in range(64):
        for c in range(2):
            south = 65 + u if c == 0 else 64 + u
            for odd in range(2):
                out[odd, c, u, 63 - u] += 1.0
                if south < 128:
                    out[odd, c, u, south] += -1.0 if odd else 1.0
    arrival = np.arange(128)
    y_source, x_source = arrival // 8, arrival % 8
    owner = (x_source // 4) * 64 + y_source * 4 + x_source % 4
    return out.reshape(256, 128)[:, owner].astype(np.float32)


EQUATOR_ROW = 4


def fourier_body(owner, own_ref, own_ids_ref, own_mask_ref, got_ref, got_ids_ref, got_mask_ref, one_ref, twist_ref, two_ref, logs_ref, out_ref):
    slot = lax.broadcasted_iota(jnp.int32, (16, 16), 0) + owner * 16
    pick_own = jnp.where(own_ids_ref[...] == slot, own_mask_ref[...], 0).astype(F32)
    pick_got = jnp.where(got_ids_ref[...] == slot, got_mask_ref[...], 0).astype(F32)
    rows = jnp.dot(pick_own, own_ref[...], precision=HIGHEST, preferred_element_type=F32) + jnp.dot(
        pick_got, got_ref[...], precision=HIGHEST, preferred_element_type=F32
    )
    folded = jnp.concatenate(
        [
            jnp.concatenate([rows[8 * c : 8 * c + 8, 128 * p : 128 * p + 128] for p in range(8)], axis=0)
            for c in range(2)
        ],
        axis=1,
    )
    first = jnp.dot(one_ref[...], folded, precision=HIGHEST, preferred_element_type=F32)
    k1 = lax.broadcasted_iota(jnp.int32, (64, 64), 1)
    row = lax.broadcasted_iota(jnp.int32, (64, 64), 0)
    orders = (k1 + 64 * jnp.where(row < 32, row, 95 - row)).astype(F32)
    outs = []
    for c in range(2):
        re, im = first[0:64, 128 * c : 128 * c + 128], first[64:128, 128 * c : 128 * c + 128]
        cos, sin = twist_ref[c, 0], twist_ref[c, 1]
        turned = jnp.concatenate([re * cos + im * sin, im * cos - re * sin], axis=1)
        spec = lax.dot_general(
            two_ref[c], turned, (((1,), (1,)), ((), ())), precision=HIGHEST, preferred_element_type=F32
        )
        seed = jnp.exp(orders * logs_ref[owner * 2 + c])
        outs.append((spec[0:64] * seed, spec[64:128] * seed))
    for j in range(4):
        pieces = []
        for ri in range(2):
            for half in range(2):
                jj = j if half == 0 else 3 - j
                for c in range(2):
                    pieces.append(outs[c][ri][32 * half : 32 * half + 32, 16 * jj : 16 * jj + 16])
        out_ref[2 * j : 2 * j + 2] = jnp.concatenate(pieces, axis=1).reshape(2, 16, 128)


def pieces_of(value):
    high = value.astype(BF16)
    rest = value - high.astype(F32)
    middle = rest.astype(BF16)
    return high, middle, (rest - middle.astype(F32)).astype(BF16)


def lane_groups():
    row = lax.broadcasted_iota(jnp.int32, (16, 128), 0)
    lane = lax.broadcasted_iota(jnp.int32, (16, 128), 1)
    return jnp.where(lane % 16 == row, 1.0, 0.0).astype(BF16)


def grouped(groups, pieces):
    total = None
    for piece in pieces:
        part = lax.dot_general(groups, piece, (((1,), (1,)), ((), ())), preferred_element_type=F32)
        total = part if total is None else total + part
    return total


def compact_tables(d, low_ref, high_ref, coef_ref, gain_ref):
    row = lax.broadcasted_iota(jnp.int32, (8, 128), 0)
    lane = lax.broadcasted_iota(jnp.int32, (8, 128), 1)
    order = lane % 16
    offset = 8 * row + lane // 16
    for half in range(2):
        first = first_order(d, half)
        start = 0 if half == 0 else 512 - 2 * d

        def one(k, carry):
            low = low_ref[pl.ds(pl.multiple_of(8 * k, 8), 8), :]
            high = high_ref[pl.ds(first // 4 + 8 * k, 8), :]
            both = low * high
            t = offset + 64 * k
            degree = t + first
            down = t - order
            up = (degree + first + order).astype(F32)
            weight = jnp.where(first + order == 0, 1.0, 2.0) * (1.0 / (CYCLES * CYCLE_PIX))
            denom = jnp.maximum(down.astype(F32), 1.0) * jnp.maximum(up, 1.0) * both
            at = pl.ds(start + 8 * k, 8)
            coef_ref[at, :] = both * (2 * degree - 1).astype(F32)
            gain_ref[at, :] = jnp.where(down >= 0, weight / jnp.where(down >= 0, denom, 1.0), 0.0)
            return carry

        lax.fori_loop(0, (4096 - first + 63) // 64, one, 0)


def spread_coef(coef_ref, spread_ref, wide_ref):
    spread = spread_ref[...]
    for chunk in range(4):
        at = pl.ds(ROWS // 4 * chunk, ROWS // 4)
        total = None
        for piece in pieces_of(coef_ref[at, :]):
            part = jnp.dot(piece, spread, preferred_element_type=F32)
            total = part if total is None else total + part
        for step in range(8):
            wide_ref[step, at, :] = total[:, 128 * step : 128 * step + 128]


def spread_gain(gain_ref, turned_ref):
    groups = lane_groups()
    row = lax.broadcasted_iota(jnp.int32, (8, 128), 0)
    lane = lax.broadcasted_iota(jnp.int32, (8, 128), 1)
    same = lane // 16 == row

    def one(tile, carry):
        rows = [
            jnp.where(same, jnp.broadcast_to(gain_ref[pl.ds(16 * tile + n, 1), :], (8, 128)), 0.0) for n in range(16)
        ]
        turned_ref[tile] = grouped(groups, pieces_of(jnp.concatenate(rows, axis=0)))
        return carry

    lax.fori_loop(0, TILES, one, 0)


def prepare(got_ref, fold_ref, state_ref):
    row = lax.broadcasted_iota(jnp.int32, (64, 128), 0)
    lane = lax.broadcasted_iota(jnp.int32, (64, 128), 1)
    got = got_ref[...].reshape(128, 128)
    folded = jnp.dot(fold_ref[...], got, precision=HIGHEST, preferred_element_type=F32)
    is_c0 = (lane % 32) < 16
    even = jnp.where(is_c0, folded[0:64], folded[64:128])
    odd = jnp.where(is_c0, folded[128:192], folded[192:256])
    same = (lane % 2) == 0
    by_parity = (jnp.where(same, even, odd), jnp.where(same, odd, even))
    group = lax.broadcasted_iota(jnp.int32, (8, 128), 1) // 32
    for half in range(2):
        for p in range(2):
            for ri in range(2):
                source = 2 * ri + half
                for v in range(2):
                    total = None
                    for h in range(4):
                        piece = by_parity[p][32 * v + 8 * h : 32 * v + 8 * h + 8]
                        moved = pltpu.roll(piece, (32 * (h - source)) % 128, 1)
                        total = moved if total is None else jnp.where(group == h, moved, total)
                    state_ref[half, 4 * p + 2 * ri + v] = total
    step = lax.broadcasted_iota(jnp.int32, (8, 128), 0)
    lane8 = lax.broadcasted_iota(jnp.int32, (8, 128), 1)
    turn = (step - lane8 % 16) & 3
    sign = jnp.where(turn == 0, 1.0, jnp.where(turn == 2, -1.0, 0.0))
    line = jnp.broadcast_to(got[EQUATOR_ROW : EQUATOR_ROW + 1, :], (8, 128))
    for half in range(2):
        for ri in range(2):
            source = 2 * ri + half
            base = jnp.where(lane8 // 16 == 2 * source, line, 0.0)
            base = pltpu.roll(base, (128 - 32 * source) % 128, 1)
            state_ref[half, 8 + ri] = base * sign


def first_order(d, half):
    return 16 * d if half == 0 else 4080 - 16 * d


UNROLL = 8


def legendre_body(d, coef_ref, state_ref, raw_ref):
    row = lax.broadcasted_iota(jnp.int32, (8, 128), 0)
    lane = lax.broadcasted_iota(jnp.int32, (8, 128), 1)
    order = lane % 16
    masks = ((row & 1) == 0, (row & 2) == 0, (row & 4) == 0)
    lats = []
    for v in range(2):
        u = 32 * v + 8 * (lane // 32) + row
        q = 2 * u + jnp.where((lane % 32) < 16, 2, 1)
        lats.append(q.astype(F32) * (2.0 / (3.0 * NSIDE)))

    def merge(level, first, second):
        mask = masks[level]
        shift = 8 - (1 << level)
        return jnp.where(mask, first, second) + pltpu.roll(jnp.where(mask, second, first), shift, 0)

    def eight(base, weights, state, seeded, k):
        a0, a1, b0, b1 = state
        stack = {}
        for step in range(8):
            coef = jnp.broadcast_to(coef_ref[step, pl.ds(base + k, 1), :], (8, 128))
            n0 = (coef * lats[0]) * a0 - b0
            n1 = (coef * lats[1]) * a1 - b1
            if seeded is not None:
                start = order == (seeded * 8 + step)
                n0 = jnp.where(start, 1.0, n0)
                n1 = jnp.where(start, 1.0, n1)
            a0, a1, b0, b1 = n0, n1, a0, a1
            p = step % 2
            for ri in range(2):
                term = n0 * weights[4 * p + 2 * ri] + n1 * weights[4 * p + 2 * ri + 1]
                level, idx = 0, step
                while idx % 2 == 1:
                    term = merge(level, stack.pop((ri, level)), term)
                    level, idx = level + 1, idx // 2
                stack[(ri, level)] = term
        for ri in range(2):
            raw_ref[ri, base + k] = stack[(ri, 3)] + weights[8 + ri]
        return (a0, a1, b0, b1)

    for half in range(2):
        first = first_order(d, half)
        base = 0 if half == 0 else 512 - 2 * d
        weights = [state_ref[half, n] for n in range(10)]
        zero = jnp.zeros((8, 128), F32)
        state = (zero, zero, zero, zero)
        for k in range(2):
            state = eight(base, weights, state, k, k)
        def many(n, state):
            for k in range(UNROLL):
                state = eight(base, weights, state, None, UNROLL * n + k + 2)
            return state

        lax.fori_loop(0, ((4096 - first) // 8 - 2 + UNROLL - 1) // UNROLL, many, state)


def power_body(d, raw_ref, turned_ref, rows_ref, shift_ref):
    groups = lane_groups()

    def one(tile, carry):
        total = None
        for ri in range(2):
            value = raw_ref[ri, pl.ds(pl.multiple_of(16 * tile, 16), 16)].reshape(128, 128)
            value = grouped(groups, pieces_of(value))
            total = value * value if total is None else total + value * value
        rows_ref[pl.ds(tile, 1), :] = jnp.sum(total * turned_ref[tile], axis=0, keepdims=True)
        return carry

    def several(n, carry):
        for k in range(POWER_UNROLL):
            one(POWER_UNROLL * n + k, carry)
        return carry

    lax.fori_loop(0, TILES // POWER_UNROLL, several, 0)
    bound = 4096 - 16 * d
    step = 128 * lax.broadcasted_iota(jnp.int32, (40, 128), 0) + lax.broadcasted_iota(jnp.int32, (40, 128), 1)
    rows = rows_ref[...]
    shift_ref[0:32, :] = jnp.zeros((32, 128), F32)
    shift_ref[32:72, :] = pltpu.roll(jnp.where(step < bound, rows, 0.0), 16 * (d % 8), 1)
    later = pltpu.roll(jnp.where((step >= bound) & (step < 4112), rows, 0.0), 112, 1)
    lane = lax.broadcasted_iota(jnp.int32, (32, 128), 1)
    near = shift_ref[pl.ds(32 - d // 8, 32), :]
    far = shift_ref[pl.ds(31 - d // 8, 32), :]
    return jnp.where(lane >= 16 * (d % 8), near, far) + jnp.where(lane < 112, later[0:32], later[1:33])


def position():
    blk, mblk = lax.axis_index("blk"), lax.axis_index("mblk")
    return blk * 4 + mblk % 4, mblk // 4


def device_at(x, y):
    return (x // 4, y * 4 + x % 4)


def order_block(rank):
    return 4 * (rank % 32) + rank // 32


def greet(x, y):
    barrier = pltpu.get_barrier_semaphore()
    for step in range(1, 8):
        pl.semaphore_signal(barrier, inc=1, device_id=device_at((x + step) % 8, y), device_id_type=MESH)
    for step in range(1, 16):
        pl.semaphore_signal(barrier, inc=1, device_id=device_at(x, (y + step) % 16), device_id_type=MESH)
    pl.semaphore_wait(barrier, 22)


def send(source, target, send_sem, recv_sem, device):
    copy = pltpu.make_async_remote_copy(
        src_ref=source, dst_ref=target, send_sem=send_sem, recv_sem=recv_sem, device_id=device, device_id_type=MESH
    )
    copy.start()
    return copy


def drain(ref, sem):
    pltpu.make_async_copy(ref, ref, sem).wait()


def everything(
    own_ref, own_ids_ref, own_mask_ref, model_ref, logs_ref,
    one_hbm, twist_hbm, two_hbm, low_hbm, high_hbm, spread_hbm, fold_hbm,
    pseudo_ref, misfit_ref,
    one_ref, twist_ref, two_ref, low_ref, high_ref, spread_ref, fold_ref, local_sem,
    got_ref, got_ids_ref, got_mask_ref, rows_ref, mid_ref, again_ref, land_ref,
    coef_ref, gain_ref, wide_ref, turned_ref, state_ref, raw_ref, sums_ref, shift_ref,
    part_ref, first_ref, second_ref, third_ref,
    pair_send, pair_recv, send_sem, recv_sem,
):
    x, y = position()
    d = order_block(x * 16 + y)
    owner = (x // 4) * 64 + y * 4 + x % 4
    loads = [
        pltpu.make_async_copy(source, target, local_sem.at[n])
        for n, (source, target) in enumerate(
            (
                (one_hbm, one_ref), (twist_hbm, twist_ref), (two_hbm, two_ref), (low_hbm, low_ref),
                (high_hbm, high_ref), (spread_hbm, spread_ref), (fold_hbm, fold_ref),
            )
        )
    ]
    greet(x, y)
    for copy in loads:
        copy.start()
    partner = device_at((x + 4) % 8, y)
    pair = [
        send(source, target, pair_send.at[n], pair_recv.at[n], partner)
        for n, (source, target) in enumerate(
            ((own_ref, got_ref), (own_ids_ref, got_ids_ref), (own_mask_ref, got_mask_ref))
        )
    ]
    for copy in loads:
        copy.wait()
    compact_tables(d, low_ref, high_ref, coef_ref, gain_ref)
    for copy in pair:
        copy.wait()
    fourier_body(
        owner, own_ref, own_ids_ref, own_mask_ref, got_ref, got_ids_ref, got_mask_ref,
        one_ref, twist_ref, two_ref, logs_ref, rows_ref,
    )
    for step in range(1, 8):
        to = (x + step) % 8
        send(rows_ref.at[to], mid_ref.at[x], send_sem.at[0], recv_sem.at[0], device_at(to, y))
    mid_ref[x] = rows_ref[x]
    spread_coef(coef_ref, spread_ref, wide_ref)
    drain(mid_ref.at[pl.ds(0, 7)], recv_sem.at[0])
    every = mid_ref[...]
    for to in range(16):
        again_ref[to] = jnp.concatenate([every[n, to : to + 1, :] for n in range(8)], axis=0)
    for step in range(1, 16):
        to = (y + step) % 16
        send(again_ref.at[to], land_ref.at[y], send_sem.at[1], recv_sem.at[1], device_at(x, to))
    land_ref[y] = again_ref[y]
    spread_gain(gain_ref, turned_ref)
    drain(land_ref.at[pl.ds(0, 15)], recv_sem.at[1])
    prepare(land_ref, fold_ref, state_ref)
    legendre_body(d, wide_ref, state_ref, raw_ref)
    power = power_body(d, raw_ref, turned_ref, sums_ref, shift_ref)
    for n in range(8):
        part_ref[n, 0:4, :] = power[4 * n : 4 * n + 4, :]
        part_ref[n, 4:8, :] = jnp.zeros((4, 128), F32)
    for step in range(1, 8):
        to = (x + step) % 8
        send(part_ref.at[to], first_ref.at[x], send_sem.at[2], recv_sem.at[2], device_at(to, y))
    first_ref[x] = part_ref[x]
    drain(first_ref.at[pl.ds(0, 7)], recv_sem.at[2])
    second_ref[y] = jnp.sum(first_ref[...], axis=0)
    for step in range(1, 16):
        to = (y + step) % 16
        send(second_ref.at[y], second_ref.at[y], send_sem.at[3], recv_sem.at[3], device_at(x, to))
    drain(second_ref.at[pl.ds(0, 15)], recv_sem.at[3])
    third_ref[x] = jnp.sum(second_ref[...], axis=0)
    for step in range(1, 8):
        to = (x + step) % 8
        send(third_ref.at[x], third_ref.at[x], send_sem.at[4], recv_sem.at[4], device_at(to, y))
    drain(third_ref.at[pl.ds(0, 7)], recv_sem.at[4])
    total = jnp.zeros((1, 1), F32)
    for n in range(8):
        pseudo = third_ref[n, 0:4, :]
        model = model_ref[4 * n : 4 * n + 4, :]
        pseudo_ref[4 * n : 4 * n + 4, :] = pseudo
        rel_error = (pseudo - model) / model
        total = total + jnp.sum(rel_error * rel_error, keepdims=True)
    misfit_ref[...] = total * (1.0 / LMAX)
    drain(mid_ref.at[pl.ds(0, 7)], send_sem.at[0])
    drain(land_ref.at[pl.ds(0, 15)], send_sem.at[1])
    drain(first_ref.at[pl.ds(0, 7)], send_sem.at[2])
    drain(second_ref.at[pl.ds(0, 15)], send_sem.at[3])
    drain(third_ref.at[pl.ds(0, 7)], send_sem.at[4])


VM = pl.BlockSpec(memory_space=pltpu.VMEM)
SM = pl.BlockSpec(memory_space=pltpu.SMEM)
HB = pl.BlockSpec(memory_space=pl.ANY)


def on_device(pixels, block_ids, block_mask, model_cl):
    one, twist, two = dft_tables()
    low, high = degree_tables()
    spread = np.arange(128)[:, None] == 16 * (np.arange(1024) // 128) + np.arange(1024) % 16
    tables = (one, twist, two, low, high, spread.astype(jnp.bfloat16), fold_matrix())
    dma = pltpu.SemaphoreType.DMA
    pseudo_cl, misfit = pl.pallas_call(
        everything,
        out_shape=(jax.ShapeDtypeStruct((32, 128), F32), jax.ShapeDtypeStruct((1, 1), F32)),
        in_specs=[VM] * 4 + [SM] + [HB] * 7,
        out_specs=(VM, VM),
        scratch_shapes=[pltpu.VMEM(table.shape, table.dtype) for table in tables]
        + [
            dma((7,)),
            pltpu.VMEM((16, BLOCK_PIX), F32),
            pltpu.VMEM((1, 16), jnp.int32),
            pltpu.VMEM((1, 16), jnp.int32),
            pltpu.VMEM((8, 16, 128), F32),
            pltpu.VMEM((8, 16, 128), F32),
            pltpu.VMEM((16, 8, 128), F32),
            pltpu.VMEM((16, 8, 128), F32),
            pltpu.VMEM((ROWS, 128), F32),
            pltpu.VMEM((ROWS, 128), F32),
            pltpu.VMEM((8, ROWS, 128), F32),
            pltpu.VMEM((TILES, 16, 128), F32),
            pltpu.VMEM((2, 10, 8, 128), F32),
            pltpu.VMEM((2, 528, 8, 128), F32),
            pltpu.VMEM((40, 128), F32),
            pltpu.VMEM((72, 128), F32),
            pltpu.VMEM((8, 8, 128), F32),
            pltpu.VMEM((8, 8, 128), F32),
            pltpu.VMEM((16, 8, 128), F32),
            pltpu.VMEM((8, 8, 128), F32),
            dma((3,)),
            dma((3,)),
            dma((5,)),
            dma((5,)),
        ],
        compiler_params=pltpu.CompilerParams(
            collective_id=0, has_side_effects=True, vmem_limit_bytes=56 * 1024 * 1024
        ),
    )(pixels, block_ids.reshape(1, 16), block_mask.reshape(1, 16), model_cl.reshape(32, 128), half_logs(), *tables)
    return pseudo_cl.reshape(LMAX), misfit.reshape(())


def solution(mesh):
    in_specs = (P(("blk", "mblk"), None), P(("blk", "mblk")), P(("blk", "mblk")), P())
    return jax.shard_map(on_device, mesh=mesh, in_specs=in_specs, out_specs=(P(), P()), check_vma=False)
```

```python
import functools
import math

import jax
import jax.numpy as jnp
import numpy as np
from jax import lax
from jax.experimental import pallas as pl
from jax.experimental.pallas import tpu as pltpu
from jax.sharding import PartitionSpec as P

NSIDE = 2048
CYCLE_PIX = 8192
LMAX = 4096
BLOCK_PIX = 1024
CYCLES = 256
DEVICES = 128
MESH = pl.DeviceIdType.MESH
HIGHEST = lax.Precision.HIGHEST
F32 = jnp.float32
BF16 = jnp.bfloat16
ROWS = 544
TILES = 33
CUTS = (20, 75)


def dft_tables():
    k1 = np.arange(64)
    part, seg = np.meshgrid(np.arange(8), np.arange(8), indexing="ij")
    outer = (8 * seg + part).reshape(-1)
    angle = 2.0 * np.pi * ((k1[:, None] * outer[None, :]) % 64) / 64
    stage_one = np.concatenate([np.cos(angle), -np.sin(angle)], axis=0)
    inner = np.arange(128)
    twists = []
    stage_two = []
    upper = np.concatenate([np.arange(32), 63 - np.arange(32)])
    for cycle in range(2):
        shift = 0.5 if cycle == 0 else 0.0
        turn = 2.0 * np.pi * (k1[:, None] * (inner[None, :] + shift)) / CYCLE_PIX
        twists.append(np.stack([np.cos(turn), np.sin(turn)]))
        turn = 2.0 * np.pi * (upper[:, None] * inner[None, :] % 128) / 128 + (
            2.0 * np.pi * upper[:, None] * shift / 128
        )
        cos_two, sin_two = np.cos(turn), np.sin(turn)
        stage_two.append(
            np.concatenate(
                [
                    np.concatenate([cos_two, sin_two], axis=1),
                    np.concatenate([-sin_two, cos_two], axis=1),
                ],
                axis=0,
            )
        )
    return (
        stage_one.astype(np.float32),
        np.stack(twists).astype(np.float32),
        np.stack(stage_two).astype(np.float32),
    )


def half_logs():
    lat = (CYCLES // 2 - np.arange(CYCLES)) * (2.0 / (3.0 * NSIDE))
    return (0.5 * np.log1p(-lat * lat)).astype(np.float32)


def ratio_table():
    steps = np.arange(1, 4200, dtype=np.float64)
    prods = np.concatenate([[1.0], np.cumprod((2.0 * steps - 1.0) / (2.0 * steps))])
    j = np.arange(8384)
    even = 1.0 / (np.maximum(j, 1) * prods[j // 2])
    odd = prods[np.maximum(j - 1, 0) // 2]
    f = np.where(j % 2 == 0, even, odd)
    f[0] = 1.0
    return f


def degree_tables():
    f = ratio_table()
    step, lane = np.arange(128) // 16, np.arange(128) % 16
    diff = 8 * np.arange(528)[:, None] + (step - lane)[None, :]
    low = np.where(diff >= 0, f[np.maximum(diff, 0)], 0.0)
    high = f[8 * np.arange(1040)[:, None] + (step + lane)[None, :]]
    return low.astype(np.float32), high.astype(np.float32)


def fold_matrix():
    out = np.zeros((2, 2, 64, 128))
    for u in range(64):
        for c in range(2):
            south = 65 + u if c == 0 else 64 + u
            for odd in range(2):
                out[odd, c, u, 63 - u] += 1.0
                if south < 128:
                    out[odd, c, u, south] += -1.0 if odd else 1.0
    arrival = np.arange(128)
    y_source, x_source = arrival // 8, arrival % 8
    owner = (x_source // 4) * 64 + y_source * 4 + x_source % 4
    return out.reshape(256, 128)[:, owner].astype(np.float32)


EQUATOR_ROW = 4


def fourier_body(pair, ids_ref, mask_ref, own_ref, one_ref, twist_ref, two_ref, logs_ref, out_ref):
    row = lax.broadcasted_iota(jnp.int32, (32, 16), 0)
    slot = (pair + 64 * (row // 16)) * 16 + row % 16
    pick = jnp.where(ids_ref[...] == slot, mask_ref[...], 0).astype(F32)
    rows = jnp.dot(pick, own_ref[...], precision=HIGHEST, preferred_element_type=F32)
    folded = jnp.concatenate(
        [
            jnp.concatenate([rows[8 * n : 8 * n + 8, 128 * p : 128 * p + 128] for p in range(8)], axis=0)
            for n in range(4)
        ],
        axis=1,
    )
    first = jnp.dot(one_ref[...], folded, precision=HIGHEST, preferred_element_type=F32)
    k1 = lax.broadcasted_iota(jnp.int32, (64, 64), 1)
    upper = lax.broadcasted_iota(jnp.int32, (64, 64), 0)
    orders = (k1 + 64 * jnp.where(upper < 32, upper, 95 - upper)).astype(F32)
    outs = [[None, None], [None, None]]
    for c in range(2):
        cos, sin = twist_ref[c, 0], twist_ref[c, 1]
        turned = []
        for band in range(2):
            lanes = slice(128 * (2 * band + c), 128 * (2 * band + c) + 128)
            re, im = first[0:64, lanes], first[64:128, lanes]
            turned.append(jnp.concatenate([re * cos + im * sin, im * cos - re * sin], axis=1))
        spec = lax.dot_general(
            two_ref[c],
            jnp.concatenate(turned, axis=0),
            (((1,), (1,)), ((), ())),
            precision=HIGHEST,
            preferred_element_type=F32,
        )
        for band in range(2):
            seed = jnp.exp(orders * logs_ref[2 * (pair + 64 * band) + c])
            lanes = slice(64 * band, 64 * band + 64)
            outs[band][c] = (spec[0:64, lanes] * seed, spec[64:128, lanes] * seed)
    for band in range(2):
        for j in range(4):
            pieces = []
            for ri in range(2):
                for half in range(2):
                    jj = j if half == 0 else 3 - j
                    for c in range(2):
                        pieces.append(outs[band][c][ri][32 * half : 32 * half + 32, 16 * jj : 16 * jj + 16])
            joined = jnp.concatenate(pieces, axis=1)
            for n in range(2):
                out_ref[2 * j + n, band] = joined[16 * n : 16 * n + 16]


def two_pieces(value):
    high = value.astype(BF16)
    return jnp.concatenate([high, (value - high.astype(F32)).astype(BF16)], axis=1)


def pieces_of(value):
    high = value.astype(BF16)
    rest = value - high.astype(F32)
    middle = rest.astype(BF16)
    return high, middle, (rest - middle.astype(F32)).astype(BF16)


def blocks_before(d):
    return 512 - 16 * (d // 8)


def compact_tables(d, low_ref, high_ref, coef_ref, gain_ref):
    row = lax.broadcasted_iota(jnp.int32, (8, 128), 0)
    lane = lax.broadcasted_iota(jnp.int32, (8, 128), 1)
    order = lane % 16
    offset = 8 * row + lane // 16
    coef_ref[...] = jnp.zeros((ROWS, 128), F32)
    gain_ref[...] = jnp.zeros((ROWS, 128), F32)
    for half in range(2):
        first = first_order(d, half)
        start = 0 if half == 0 else blocks_before(d)

        def one(k, carry):
            low = low_ref[pl.ds(pl.multiple_of(8 * k, 8), 8), :]
            high = high_ref[pl.ds(first // 4 + 8 * k, 8), :]
            both = low * high
            t = offset + 64 * k
            degree = t + first
            down = t - order
            up = (degree + first + order).astype(F32)
            weight = jnp.where(first + order == 0, 1.0, 2.0) * (1.0 / (CYCLES * CYCLE_PIX))
            denom = jnp.maximum(down.astype(F32), 1.0) * jnp.maximum(up, 1.0) * both
            at = pl.ds(start + 8 * k, 8)
            coef_ref[at, :] = both * (2 * degree - 1).astype(F32)
            gain_ref[at, :] = jnp.where(down >= 0, weight / jnp.where(down >= 0, denom, 1.0), 0.0)
            return carry

        lax.fori_loop(0, (4096 - first + 63) // 64, one, 0)


def spread_coef(coef_ref, spread_ref, wide_ref):
    spread = spread_ref[...]
    for chunk in range(4):
        at = pl.ds(ROWS // 4 * chunk, ROWS // 4)
        total = None
        for piece in pieces_of(coef_ref[at, :]):
            part = jnp.dot(piece, spread, preferred_element_type=F32)
            total = part if total is None else total + part
        for step in range(8):
            wide_ref[step, at, :] = total[:, 128 * step : 128 * step + 128]


def spread_gain(gain_ref, spread_ref, wide_ref, gains_ref):
    spread = jnp.concatenate([spread_ref[...]] * 2, axis=0)
    for chunk in range(4):
        start = ROWS // 4 * chunk
        total = jnp.dot(two_pieces(gain_ref[pl.ds(start, ROWS // 4), :]), spread, preferred_element_type=F32)
        for step in range(8):
            wide_ref[pl.ds(8 * start + step, ROWS // 4, stride=8), :] = total[:, 128 * step : 128 * step + 128]
    quarter = lax.broadcasted_iota(jnp.int32, (8, 128), 1) // 16 % 4

    def one(tile, carry):
        for n in range(4):
            packed = None
            for q in range(4):
                rows = wide_ref[pl.ds(pl.multiple_of(128 * tile + 32 * q + 8 * n, 8), 8), :]
                packed = rows if packed is None else jnp.where(quarter == q, rows, packed)
            gains_ref[4 * tile + n] = packed
        return carry

    lax.fori_loop(0, TILES, one, 0)


def prepare(got_ref, fold_ref, state_ref):
    row = lax.broadcasted_iota(jnp.int32, (64, 128), 0)
    lane = lax.broadcasted_iota(jnp.int32, (64, 128), 1)
    got = got_ref[...].reshape(128, 128)
    folded = jnp.dot(fold_ref[...], got, precision=HIGHEST, preferred_element_type=F32)
    is_c0 = (lane % 32) < 16
    even = jnp.where(is_c0, folded[0:64], folded[64:128])
    odd = jnp.where(is_c0, folded[128:192], folded[192:256])
    same = (lane % 2) == 0
    by_parity = (jnp.where(same, even, odd), jnp.where(same, odd, even))
    group = lax.broadcasted_iota(jnp.int32, (8, 128), 1) // 32
    for half in range(2):
        for p in range(2):
            for ri in range(2):
                source = 2 * ri + half
                for v in range(2):
                    total = None
                    for h in range(4):
                        piece = by_parity[p][32 * v + 8 * h : 32 * v + 8 * h + 8]
                        moved = pltpu.roll(piece, (32 * (h - source)) % 128, 1)
                        total = moved if total is None else jnp.where(group == h, moved, total)
                    state_ref[half, 4 * p + 2 * ri + v] = total
    step = lax.broadcasted_iota(jnp.int32, (8, 128), 0)
    lane8 = lax.broadcasted_iota(jnp.int32, (8, 128), 1)
    turn = (step - lane8 % 16) & 3
    sign = jnp.where(turn == 0, 1.0, jnp.where(turn == 2, -1.0, 0.0))
    line = jnp.broadcast_to(got[EQUATOR_ROW : EQUATOR_ROW + 1, :], (8, 128))
    for half in range(2):
        for ri in range(2):
            source = 2 * ri + half
            base = jnp.where(lane8 // 16 == 2 * source, line, 0.0)
            base = pltpu.roll(base, (128 - 32 * source) % 128, 1)
            state_ref[half, 8 + ri] = base * sign


def first_order(d, half):
    return 16 * d if half == 0 else 4080 - 16 * d


def first_order(d, half):
    return 16 * d if half == 0 else 4080 - 16 * d


def latitudes():
    row = lax.broadcasted_iota(jnp.int32, (8, 128), 0)
    lane = lax.broadcasted_iota(jnp.int32, (8, 128), 1)
    lats = []
    for v in range(2):
        u = 32 * v + 8 * (lane // 32) + row
        q = 2 * u + jnp.where((lane % 32) < 16, 2, 1)
        lats.append(q.astype(F32) * (2.0 / (3.0 * NSIDE)))
    return lats


def value_of(order, fresh, step):
    return jnp.where(order == step, fresh, 0.0)


def recur(d, coef_ref, values_ref, low, top, state):
    order = lax.broadcasted_iota(jnp.int32, (8, 128), 1) % 16
    lats = latitudes()
    restart = blocks_before(d) // 4

    def quad(n, state):
        fresh = jnp.where((n == 0) | (n == restart), 1.0, 0.0)
        a0, a1, b0, b1 = [value * (1.0 - fresh) for value in state]
        for step in range(0, 32, 2):
            block = 4 * n + step // 8
            now, later = [
                jnp.broadcast_to(coef_ref[(step + k) % 8, pl.ds(block, 1), :], (8, 128)) for k in range(2)
            ]
            ones = [value_of(order, fresh, step + k) for k in range(2)] if step < 16 else None
            fresh_pair = []
            for v, (one_back, two_back) in enumerate(((a0, b0), (a1, b1))):
                c0, c1 = now * lats[v], later * lats[v]
                if ones is not None:
                    two_back = two_back - ones[0]
                rest = c1 * two_back
                if ones is not None:
                    rest = rest - ones[1]
                first = c0 * one_back - two_back
                second = (c1 * c0 - 1.0) * one_back - rest
                values_ref[block, v, pl.ds(step % 8, 8, stride=8), :] = first
                values_ref[block, v, pl.ds(step % 8 + 1, 8, stride=8), :] = second
                fresh_pair.append((second, first))
            (a0, b0), (a1, b1) = fresh_pair
        return (a0, a1, b0, b1)

    return lax.fori_loop(low, top, quad, state)


def widen_weights(state_ref, weights_ref):
    even_row = (lax.broadcasted_iota(jnp.int32, (8, 128), 0) & 1) == 0
    for half in range(2):
        for v in range(2):
            for ri in range(2):
                even, odd = state_ref[half, 2 * ri + v], state_ref[half, 4 + 2 * ri + v]
                for s in range(8):
                    weights_ref[half, v, s, ri] = jnp.where(
                        even_row,
                        jnp.broadcast_to(even[s : s + 1], (8, 128)),
                        jnp.broadcast_to(odd[s : s + 1], (8, 128)),
                    )


def contract(d, values_ref, weights_ref, state_ref, gains_ref, squares_ref, tile):
    lane = lax.broadcasted_iota(jnp.int32, (8, 128), 1)
    masks = {shift: (lane & shift) == 0 for shift in (16, 32, 64)}

    def merge(shift, first, second):
        mask = masks[shift]
        return jnp.where(mask, first, second) + pltpu.roll(jnp.where(mask, second, first), 128 - shift, 1)

    half = jnp.where(16 * tile >= blocks_before(d), 1, 0)
    for n in range(4):
        blocks = [16 * tile + n + 4 * q for q in range(4)]
        sums = [[state_ref[half, 8 + ri]] * 4 for ri in range(2)]
        for v in range(2):
            for s in range(8):
                weights = [weights_ref[half, v, s, ri] for ri in range(2)]
                for q in range(4):
                    value = values_ref[blocks[q], v, 8 * s : 8 * s + 8, :]
                    for ri in range(2):
                        sums[ri][q] = sums[ri][q] + value * weights[ri]
        parts = [
            merge(32, merge(16, sums[ri][0], sums[ri][1]), merge(16, sums[ri][2], sums[ri][3])) for ri in range(2)
        ]
        packed = merge(64, parts[0], parts[1])
        squares_ref[4 * tile + n] = packed * packed * gains_ref[4 * tile + n]


def power_body(d, values_ref, weights_ref, state_ref, gains_ref, squares_ref, columns_ref, turned_ref, shift_ref):
    def one(tile, carry):
        contract(d, values_ref, weights_ref, state_ref, gains_ref, squares_ref, tile)
        return carry

    def many(k, carry):
        for n in range(3):
            one(3 * k + n, carry)
        return carry

    lax.fori_loop(0, TILES // 3, many, 0)
    row = lax.broadcasted_iota(jnp.int32, (256, 128), 0)
    column = lax.broadcasted_iota(jnp.int32, (256, 128), 1)
    quarters = jnp.where(row // 16 % 4 == column % 4, 1.0, 0.0).astype(BF16)
    columns_ref[...] = jnp.dot(
        two_pieces(squares_ref[...].reshape(32 * TILES, 128)), quarters, preferred_element_type=F32
    )
    lane = lax.broadcasted_iota(jnp.int32, (32, 128), 1)
    tables = [jnp.zeros((32, 128), F32), jnp.zeros((32, 128), F32)]
    for tile in range(TILES):
        tables[tile // 32] = jnp.where(
            lane // 4 == tile % 32, columns_ref[32 * tile : 32 * tile + 32, :], tables[tile // 32]
        )
    for n in range(2):
        table = jnp.concatenate([tables[n], jnp.zeros((96, 128), F32)], axis=0)
        turned_ref[128 * n : 128 * n + 128, :] = jnp.transpose(table)
    rows = turned_ref[pl.ds(0, 40, stride=4), :]
    for q in range(1, 4):
        rows = rows + pltpu.roll(turned_ref[pl.ds(q, 40, stride=4), :], 32 * q, 1)
    begin = 8 * blocks_before(d)
    step = 128 * lax.broadcasted_iota(jnp.int32, (40, 128), 0) + lax.broadcasted_iota(jnp.int32, (40, 128), 1)
    shift_ref[0:32, :] = jnp.zeros((32, 128), F32)
    shift_ref[32:72, :] = pltpu.roll(jnp.where(step < 4096 - 16 * d, rows, 0.0), 16 * (d % 8), 1)
    back = 16 + 16 * (d % 8)
    later = pltpu.roll(jnp.where((step >= begin) & (step < begin + 16 * d + 16), rows, 0.0), 128 - back, 1)
    lane = lax.broadcasted_iota(jnp.int32, (32, 128), 1)
    near = shift_ref[pl.ds(32 - d // 8, 32), :]
    far = shift_ref[pl.ds(31 - d // 8, 32), :]
    return jnp.where(lane >= 16 * (d % 8), near, far) + jnp.where(lane < 128 - back, later[0:32], later[1:33])


def position():
    blk, mblk = lax.axis_index("blk"), lax.axis_index("mblk")
    return blk * 4 + mblk % 4, mblk // 4


def device_at(x, y):
    return (x // 4, y * 4 + x % 4)


def order_block(rank):
    return 4 * (rank % 32) + rank // 32


def greet(x, y):
    barrier = pltpu.get_barrier_semaphore()
    for step in range(1, 8):
        pl.semaphore_signal(barrier, inc=1, device_id=device_at((x + step) % 8, y), device_id_type=MESH)
    for step in range(1, 16):
        pl.semaphore_signal(barrier, inc=1, device_id=device_at(x, (y + step) % 16), device_id_type=MESH)
    return barrier


def send(source, target, send_sem, recv_sem, device):
    copy = pltpu.make_async_remote_copy(
        src_ref=source, dst_ref=target, send_sem=send_sem, recv_sem=recv_sem, device_id=device, device_id_type=MESH
    )
    copy.start()
    return copy


def drain(ref, sem):
    pltpu.make_async_copy(ref, ref, sem).wait()


def everything(
    pixels_hbm, ids_hbm, mask_hbm, model_hbm, logs_hbm, one_hbm, twist_hbm, two_hbm, low_hbm, high_hbm, spread_hbm, fold_hbm,
    pseudo_ref, misfit_ref,
    own_ref, ids_ref, mask_ref, model_ref, logs_ref, one_ref, twist_ref, two_ref, low_ref, high_ref, spread_ref, fold_ref,
    local_sem,
    rows_ref, mid_ref, joined_ref, again_ref, land_ref,
    coef_ref, gain_ref, wide_ref, broad_ref, gains_ref, state_ref, weights_ref, values_ref, squares_ref,
    columns_ref, turned_ref, shift_ref, part_ref, first_ref, second_ref, third_ref, send_sem, recv_sem,
):
    x, y = position()
    d = order_block(x * 16 + y)
    barrier = greet(x, y)
    loads = [
        pltpu.make_async_copy(source, target, local_sem.at[n])
        for n, (source, target) in enumerate(
            (
                (low_hbm, low_ref), (high_hbm, high_ref), (spread_hbm, spread_ref), (one_hbm, one_ref),
                (twist_hbm, twist_ref), (two_hbm, two_ref), (fold_hbm, fold_ref), (pixels_hbm, own_ref),
                (ids_hbm, ids_ref), (mask_hbm, mask_ref), (model_hbm, model_ref), (logs_hbm, logs_ref),
            )
        )
    ]
    for copy in loads:
        copy.start()
    for copy in loads[0:3]:
        copy.wait()
    compact_tables(d, low_ref, high_ref, coef_ref, gain_ref)
    spread_coef(coef_ref, spread_ref, wide_ref)
    spread_gain(gain_ref, spread_ref, broad_ref, gains_ref)
    zero = jnp.zeros((8, 128), F32)
    state = recur(d, wide_ref, values_ref, 0, CUTS[0], (zero, zero, zero, zero))
    for copy in loads[3:]:
        copy.wait()
    fourier_body(y * 4 + x % 4, ids_ref, mask_ref, own_ref, one_ref, twist_ref, two_ref, logs_ref, rows_ref)
    pl.semaphore_wait(barrier, 22)
    for step in range(1, 8):
        to = (x + step) % 8
        send(rows_ref.at[to], mid_ref.at[x], send_sem.at[0], recv_sem.at[0], device_at(to, y))
    mid_ref[x] = rows_ref[x]
    state = recur(d, wide_ref, values_ref, CUTS[0], CUTS[1], state)
    drain(mid_ref.at[pl.ds(0, 7)], recv_sem.at[0])
    for band in range(2):
        for n in range(4):
            at = 64 * band + 16 * n
            joined_ref[at : at + 16, :] = mid_ref[n, band] + mid_ref[4 + n, band]
    for to in range(16):
        again_ref[to] = joined_ref[pl.ds(to, 8, stride=16), :]
    for step in range(1, 16):
        to = (y + step) % 16
        send(again_ref.at[to], land_ref.at[y], send_sem.at[1], recv_sem.at[1], device_at(x, to))
    land_ref[y] = again_ref[y]
    recur(d, wide_ref, values_ref, CUTS[1], 4 * TILES, state)
    drain(land_ref.at[pl.ds(0, 15)], recv_sem.at[1])
    prepare(land_ref, fold_ref, state_ref)
    widen_weights(state_ref, weights_ref)
    power = power_body(
        d, values_ref, weights_ref, state_ref, gains_ref, squares_ref, columns_ref, turned_ref, shift_ref
    )
    for n in range(8):
        part_ref[n, 0:4, :] = power[4 * n : 4 * n + 4, :]
        part_ref[n, 4:8, :] = jnp.zeros((4, 128), F32)
    for step in range(1, 8):
        to = (x + step) % 8
        send(part_ref.at[to], first_ref.at[x], send_sem.at[2], recv_sem.at[2], device_at(to, y))
    first_ref[x] = part_ref[x]
    drain(first_ref.at[pl.ds(0, 7)], recv_sem.at[2])
    second_ref[y] = jnp.sum(first_ref[...], axis=0)
    for step in range(1, 16):
        to = (y + step) % 16
        send(second_ref.at[y], second_ref.at[y], send_sem.at[3], recv_sem.at[3], device_at(x, to))
    drain(second_ref.at[pl.ds(0, 15)], recv_sem.at[3])
    third_ref[x] = jnp.sum(second_ref[...], axis=0)
    for step in range(1, 8):
        to = (x + step) % 8
        send(third_ref.at[x], third_ref.at[x], send_sem.at[4], recv_sem.at[4], device_at(to, y))
    drain(third_ref.at[pl.ds(0, 7)], recv_sem.at[4])
    total = jnp.zeros((1, 1), F32)
    for n in range(8):
        pseudo = third_ref[n, 0:4, :]
        model = model_ref[4 * n : 4 * n + 4, :]
        pseudo_ref[4 * n : 4 * n + 4, :] = pseudo
        rel_error = (pseudo - model) / model
        total = total + jnp.sum(rel_error * rel_error, keepdims=True)
    misfit_ref[...] = total * (1.0 / LMAX)
    drain(mid_ref.at[pl.ds(0, 7)], send_sem.at[0])
    drain(land_ref.at[pl.ds(0, 15)], send_sem.at[1])
    drain(first_ref.at[pl.ds(0, 7)], send_sem.at[2])
    drain(second_ref.at[pl.ds(0, 15)], send_sem.at[3])
    drain(third_ref.at[pl.ds(0, 7)], send_sem.at[4])


VM = pl.BlockSpec(memory_space=pltpu.VMEM)
HB = pl.BlockSpec(memory_space=pl.ANY)


def on_device(pixels, block_ids, block_mask, model_cl):
    one, twist, two = dft_tables()
    low, high = degree_tables()
    spread = np.arange(128)[:, None] == 16 * (np.arange(1024) // 128) + np.arange(1024) % 16
    tables = (one, twist, two, low, high, spread.astype(jnp.bfloat16), fold_matrix())
    dma = pltpu.SemaphoreType.DMA
    pseudo_cl, misfit = pl.pallas_call(
        everything,
        out_shape=(jax.ShapeDtypeStruct((32, 128), F32), jax.ShapeDtypeStruct((1, 1), F32)),
        in_specs=[HB] * 12,
        out_specs=(VM, VM),
        scratch_shapes=[
            pltpu.VMEM((16, BLOCK_PIX), F32),
            pltpu.VMEM((1, 16), jnp.int32),
            pltpu.VMEM((1, 16), jnp.int32),
            pltpu.VMEM((32, 128), F32),
            pltpu.SMEM((CYCLES,), F32),
        ]
        + [pltpu.VMEM(table.shape, table.dtype) for table in tables]
        + [
            dma((12,)),
            pltpu.VMEM((8, 2, 16, 128), F32),
            pltpu.VMEM((8, 2, 16, 128), F32),
            pltpu.VMEM((128, 128), F32),
            pltpu.VMEM((16, 8, 128), F32),
            pltpu.VMEM((16, 8, 128), F32),
            pltpu.VMEM((ROWS, 128), F32),
            pltpu.VMEM((ROWS, 128), F32),
            pltpu.VMEM((8, ROWS, 128), F32),
            pltpu.VMEM((8 * ROWS, 128), F32),
            pltpu.VMEM((4 * TILES, 8, 128), F32),
            pltpu.VMEM((2, 10, 8, 128), F32),
            pltpu.VMEM((2, 2, 8, 2, 8, 128), F32),
            pltpu.VMEM((16 * TILES, 2, 64, 128), F32),
            pltpu.VMEM((4 * TILES, 8, 128), F32),
            pltpu.VMEM((32 * TILES, 128), F32),
            pltpu.VMEM((256, 128), F32),
            pltpu.VMEM((72, 128), F32),
            pltpu.VMEM((8, 8, 128), F32),
            pltpu.VMEM((8, 8, 128), F32),
            pltpu.VMEM((16, 8, 128), F32),
            pltpu.VMEM((8, 8, 128), F32),
            dma((5,)),
            dma((5,)),
        ],
        compiler_params=pltpu.CompilerParams(
            collective_id=0, has_side_effects=True, vmem_limit_bytes=60 * 1024 * 1024
        ),
    )(pixels, block_ids.reshape(1, 16), block_mask.reshape(1, 16), model_cl.reshape(32, 128), half_logs(), *tables)
    return pseudo_cl.reshape(LMAX), misfit.reshape(())


def solution(mesh):
    in_specs = (P(("blk", "mblk"), None), P(("blk", "mblk")), P(("blk", "mblk")), P())
    return jax.shard_map(on_device, mesh=mesh, in_specs=in_specs, out_specs=(P(), P()), check_vma=False)
```

```python
import functools
import math

import jax
import jax.numpy as jnp
import numpy as np
from jax import lax
from jax.experimental import pallas as pl
from jax.experimental.pallas import tpu as pltpu
from jax.sharding import PartitionSpec as P

NSIDE = 2048
CYCLE_PIX = 8192
LMAX = 4096
BLOCK_PIX = 1024
CYCLES = 256
DEVICES = 128
MESH = pl.DeviceIdType.MESH
HIGHEST = lax.Precision.HIGHEST
F32 = jnp.float32
BF16 = jnp.bfloat16
ROWS = 544
TILES = 33
CUT = 55


def dft_tables():
    k1 = np.arange(64)
    part, seg = np.meshgrid(np.arange(8), np.arange(8), indexing="ij")
    outer = (8 * seg + part).reshape(-1)
    angle = 2.0 * np.pi * ((k1[:, None] * outer[None, :]) % 64) / 64
    stage_one = np.concatenate([np.cos(angle), -np.sin(angle)], axis=0)
    inner = np.arange(128)
    twists = []
    stage_two = []
    upper = np.concatenate([np.arange(32), 63 - np.arange(32)])
    for cycle in range(2):
        shift = 0.5 if cycle == 0 else 0.0
        turn = 2.0 * np.pi * (k1[:, None] * (inner[None, :] + shift)) / CYCLE_PIX
        twists.append(np.stack([np.cos(turn), np.sin(turn)]))
        turn = 2.0 * np.pi * (upper[:, None] * inner[None, :] % 128) / 128 + (
            2.0 * np.pi * upper[:, None] * shift / 128
        )
        cos_two, sin_two = np.cos(turn), np.sin(turn)
        stage_two.append(
            np.concatenate(
                [
                    np.concatenate([cos_two, sin_two], axis=1),
                    np.concatenate([-sin_two, cos_two], axis=1),
                ],
                axis=0,
            )
        )
    return (
        stage_one.astype(np.float32),
        np.stack(twists).astype(np.float32),
        np.stack(stage_two).astype(np.float32),
    )


def half_logs():
    lat = (CYCLES // 2 - np.arange(CYCLES)) * (2.0 / (3.0 * NSIDE))
    return (0.5 * np.log1p(-lat * lat)).astype(np.float32)


def ratio_table():
    steps = np.arange(1, 4200, dtype=np.float64)
    prods = np.concatenate([[1.0], np.cumprod((2.0 * steps - 1.0) / (2.0 * steps))])
    j = np.arange(8384)
    even = 1.0 / (np.maximum(j, 1) * prods[j // 2])
    odd = prods[np.maximum(j - 1, 0) // 2]
    f = np.where(j % 2 == 0, even, odd)
    f[0] = 1.0
    return f


def degree_tables():
    f = ratio_table()
    step, lane = np.arange(128) // 16, np.arange(128) % 16
    diff = 8 * np.arange(528)[:, None] + (step - lane)[None, :]
    low = np.where(diff >= 0, f[np.maximum(diff, 0)], 0.0)
    high = f[8 * np.arange(1040)[:, None] + (step + lane)[None, :]]
    return low.astype(np.float32), high.astype(np.float32)


def fold_matrix():
    out = np.zeros((2, 2, 64, 128))
    for u in range(64):
        for c in range(2):
            south = 65 + u if c == 0 else 64 + u
            for odd in range(2):
                out[odd, c, u, 63 - u] += 1.0
                if south < 128:
                    out[odd, c, u, south] += -1.0 if odd else 1.0
    arrival = np.arange(128)
    y_source, x_source = arrival // 8, arrival % 8
    owner = (x_source // 4) * 64 + y_source * 4 + x_source % 4
    return out.reshape(256, 128)[:, owner].astype(np.float32)


EQUATOR_ROW = 4


def fourier_body(pair, ids_ref, mask_ref, own_ref, one_ref, twist_ref, two_ref, logs_ref, out_ref):
    row = lax.broadcasted_iota(jnp.int32, (32, 16), 0)
    slot = (pair + 64 * (row // 16)) * 16 + row % 16
    pick = jnp.where(ids_ref[...] == slot, mask_ref[...], 0).astype(F32)
    rows = jnp.dot(pick, own_ref[...], precision=HIGHEST, preferred_element_type=F32)
    folded = jnp.concatenate(
        [
            jnp.concatenate([rows[8 * n : 8 * n + 8, 128 * p : 128 * p + 128] for p in range(8)], axis=0)
            for n in range(4)
        ],
        axis=1,
    )
    first = jnp.dot(one_ref[...], folded, precision=HIGHEST, preferred_element_type=F32)
    k1 = lax.broadcasted_iota(jnp.int32, (64, 64), 1)
    upper = lax.broadcasted_iota(jnp.int32, (64, 64), 0)
    orders = (k1 + 64 * jnp.where(upper < 32, upper, 95 - upper)).astype(F32)
    outs = [[None, None], [None, None]]
    for c in range(2):
        cos, sin = twist_ref[c, 0], twist_ref[c, 1]
        turned = []
        for band in range(2):
            lanes = slice(128 * (2 * band + c), 128 * (2 * band + c) + 128)
            re, im = first[0:64, lanes], first[64:128, lanes]
            turned.append(jnp.concatenate([re * cos + im * sin, im * cos - re * sin], axis=1))
        spec = lax.dot_general(
            two_ref[c],
            jnp.concatenate(turned, axis=0),
            (((1,), (1,)), ((), ())),
            precision=HIGHEST,
            preferred_element_type=F32,
        )
        for band in range(2):
            seed = jnp.exp(orders * logs_ref[2 * (pair + 64 * band) + c])
            lanes = slice(64 * band, 64 * band + 64)
            outs[band][c] = (spec[0:64, lanes] * seed, spec[64:128, lanes] * seed)
    for band in range(2):
        for j in range(4):
            pieces = []
            for ri in range(2):
                for half in range(2):
                    jj = j if half == 0 else 3 - j
                    for c in range(2):
                        pieces.append(outs[band][c][ri][32 * half : 32 * half + 32, 16 * jj : 16 * jj + 16])
            joined = jnp.concatenate(pieces, axis=1)
            for n in range(2):
                out_ref[2 * j + n, band] = joined[16 * n : 16 * n + 16]


def two_pieces(value):
    high = value.astype(BF16)
    return jnp.concatenate([high, (value - high.astype(F32)).astype(BF16)], axis=1)


def pieces_of(value):
    high = value.astype(BF16)
    rest = value - high.astype(F32)
    middle = rest.astype(BF16)
    return high, middle, (rest - middle.astype(F32)).astype(BF16)


def blocks_before(d):
    return 512 - 16 * (d // 8)


def compact_tables(d, low_ref, high_ref, coef_ref, gain_ref):
    row = lax.broadcasted_iota(jnp.int32, (8, 128), 0)
    lane = lax.broadcasted_iota(jnp.int32, (8, 128), 1)
    order = lane % 16
    offset = 8 * row + lane // 16
    coef_ref[...] = jnp.zeros((ROWS, 128), F32)
    gain_ref[...] = jnp.zeros((ROWS, 128), F32)
    for half in range(2):
        first = first_order(d, half)
        start = 0 if half == 0 else blocks_before(d)

        def one(k, carry):
            low = low_ref[pl.ds(pl.multiple_of(8 * k, 8), 8), :]
            high = high_ref[pl.ds(first // 4 + 8 * k, 8), :]
            both = low * high
            t = offset + 64 * k
            degree = t + first
            down = t - order
            up = (degree + first + order).astype(F32)
            weight = jnp.where(first + order == 0, 1.0, 2.0) * (1.0 / (CYCLES * CYCLE_PIX))
            denom = jnp.maximum(down.astype(F32), 1.0) * jnp.maximum(up, 1.0) * both
            at = pl.ds(start + 8 * k, 8)
            coef_ref[at, :] = both * (2 * degree - 1).astype(F32)
            gain_ref[at, :] = jnp.where(down >= 0, weight / jnp.where(down >= 0, denom, 1.0), 0.0)
            return carry

        lax.fori_loop(0, (4096 - first + 63) // 64, one, 0)


def spread_coef(coef_ref, spread_ref, wide_ref):
    spread = spread_ref[...]
    for chunk in range(4):
        at = pl.ds(ROWS // 4 * chunk, ROWS // 4)
        total = None
        for piece in pieces_of(coef_ref[at, :]):
            part = jnp.dot(piece, spread, preferred_element_type=F32)
            total = part if total is None else total + part
        for step in range(8):
            wide_ref[step, at, :] = total[:, 128 * step : 128 * step + 128]


def spread_gain(gain_ref, spread_ref, wide_ref, gains_ref):
    spread = jnp.concatenate([spread_ref[...]] * 2, axis=0)
    for chunk in range(4):
        start = ROWS // 4 * chunk
        total = jnp.dot(two_pieces(gain_ref[pl.ds(start, ROWS // 4), :]), spread, preferred_element_type=F32)
        for step in range(8):
            wide_ref[pl.ds(8 * start + step, ROWS // 4, stride=8), :] = total[:, 128 * step : 128 * step + 128]
    quarter = lax.broadcasted_iota(jnp.int32, (8, 128), 1) // 16 % 4

    def one(tile, carry):
        for n in range(4):
            packed = None
            for q in range(4):
                rows = wide_ref[pl.ds(pl.multiple_of(128 * tile + 32 * q + 8 * n, 8), 8), :]
                packed = rows if packed is None else jnp.where(quarter == q, rows, packed)
            gains_ref[4 * tile + n] = packed
        return carry

    def many(k, carry):
        for n in range(3):
            one(3 * k + n, carry)
        return carry

    lax.fori_loop(0, TILES // 3, many, 0)


def prepare(got_ref, fold_ref, state_ref):
    row = lax.broadcasted_iota(jnp.int32, (64, 128), 0)
    lane = lax.broadcasted_iota(jnp.int32, (64, 128), 1)
    got = got_ref[...].reshape(128, 128)
    folded = jnp.dot(fold_ref[...], got, precision=HIGHEST, preferred_element_type=F32)
    is_c0 = (lane % 32) < 16
    even = jnp.where(is_c0, folded[0:64], folded[64:128])
    odd = jnp.where(is_c0, folded[128:192], folded[192:256])
    same = (lane % 2) == 0
    by_parity = (jnp.where(same, even, odd), jnp.where(same, odd, even))
    group = lax.broadcasted_iota(jnp.int32, (8, 128), 1) // 32
    for half in range(2):
        for p in range(2):
            for ri in range(2):
                source = 2 * ri + half
                for v in range(2):
                    total = None
                    for h in range(4):
                        piece = by_parity[p][32 * v + 8 * h : 32 * v + 8 * h + 8]
                        moved = pltpu.roll(piece, (32 * (h - source)) % 128, 1)
                        total = moved if total is None else jnp.where(group == h, moved, total)
                    state_ref[half, 4 * p + 2 * ri + v] = total
    step = lax.broadcasted_iota(jnp.int32, (8, 128), 0)
    lane8 = lax.broadcasted_iota(jnp.int32, (8, 128), 1)
    turn = (step - lane8 % 16) & 3
    sign = jnp.where(turn == 0, 1.0, jnp.where(turn == 2, -1.0, 0.0))
    line = jnp.broadcast_to(got[EQUATOR_ROW : EQUATOR_ROW + 1, :], (8, 128))
    for half in range(2):
        for ri in range(2):
            source = 2 * ri + half
            base = jnp.where(lane8 // 16 == 2 * source, line, 0.0)
            base = pltpu.roll(base, (128 - 32 * source) % 128, 1)
            state_ref[half, 8 + ri] = base * sign


def first_order(d, half):
    return 16 * d if half == 0 else 4080 - 16 * d


def first_order(d, half):
    return 16 * d if half == 0 else 4080 - 16 * d


def latitudes():
    row = lax.broadcasted_iota(jnp.int32, (8, 128), 0)
    lane = lax.broadcasted_iota(jnp.int32, (8, 128), 1)
    lats = []
    for v in range(2):
        u = 32 * v + 8 * (lane // 32) + row
        q = 2 * u + jnp.where((lane % 32) < 16, 2, 1)
        lats.append(q.astype(F32) * (2.0 / (3.0 * NSIDE)))
    return lats


def value_of(order, fresh, step):
    return jnp.where(order == step, fresh, 0.0)


def recur(d, coef_ref, values_ref, low, top, state):
    order = lax.broadcasted_iota(jnp.int32, (8, 128), 1) % 16
    lats = latitudes()
    restart = blocks_before(d) // 4

    def quad(n, state):
        fresh = jnp.where((n == 0) | (n == restart), 1.0, 0.0)
        a0, a1, b0, b1 = [value * (1.0 - fresh) for value in state]
        for step in range(0, 32, 2):
            block = 4 * n + step // 8
            now, later = [
                jnp.broadcast_to(coef_ref[(step + k) % 8, pl.ds(block, 1), :], (8, 128)) for k in range(2)
            ]
            ones = [value_of(order, fresh, step + k) for k in range(2)] if step < 16 else None
            fresh_pair = []
            for v, (one_back, two_back) in enumerate(((a0, b0), (a1, b1))):
                c0, c1 = now * lats[v], later * lats[v]
                if ones is not None:
                    two_back = two_back - ones[0]
                rest = c1 * two_back
                if ones is not None:
                    rest = rest - ones[1]
                first = c0 * one_back - two_back
                second = (c1 * c0 - 1.0) * one_back - rest
                values_ref[block, v, pl.ds(step % 8, 8, stride=8), :] = first
                values_ref[block, v, pl.ds(step % 8 + 1, 8, stride=8), :] = second
                fresh_pair.append((second, first))
            (a0, b0), (a1, b1) = fresh_pair
        return (a0, a1, b0, b1)

    return lax.fori_loop(low, top, quad, state)


def widen_weights(state_ref, weights_ref):
    even_row = (lax.broadcasted_iota(jnp.int32, (8, 128), 0) & 1) == 0
    for half in range(2):
        for v in range(2):
            for ri in range(2):
                even, odd = state_ref[half, 2 * ri + v], state_ref[half, 4 + 2 * ri + v]
                for s in range(8):
                    weights_ref[half, v, s, ri] = jnp.where(
                        even_row,
                        jnp.broadcast_to(even[s : s + 1], (8, 128)),
                        jnp.broadcast_to(odd[s : s + 1], (8, 128)),
                    )


def contract(d, values_ref, weights_ref, state_ref, gains_ref, squares_ref, tile):
    lane = lax.broadcasted_iota(jnp.int32, (8, 128), 1)
    masks = {shift: (lane & shift) == 0 for shift in (16, 32, 64)}

    def merge(shift, first, second):
        mask = masks[shift]
        return jnp.where(mask, first, second) + pltpu.roll(jnp.where(mask, second, first), 128 - shift, 1)

    half = jnp.where(16 * tile >= blocks_before(d), 1, 0)
    for n in range(4):
        blocks = [16 * tile + n + 4 * q for q in range(4)]
        sums = [[state_ref[half, 8 + ri]] * 4 for ri in range(2)]
        for v in range(2):
            for s in range(8):
                weights = [weights_ref[half, v, s, ri] for ri in range(2)]
                for q in range(4):
                    value = values_ref[blocks[q], v, 8 * s : 8 * s + 8, :]
                    for ri in range(2):
                        sums[ri][q] = sums[ri][q] + value * weights[ri]
        parts = [
            merge(32, merge(16, sums[ri][0], sums[ri][1]), merge(16, sums[ri][2], sums[ri][3])) for ri in range(2)
        ]
        packed = merge(64, parts[0], parts[1])
        squares_ref[4 * tile + n] = packed * packed * gains_ref[4 * tile + n]


def power_body(d, values_ref, weights_ref, state_ref, gains_ref, squares_ref, columns_ref, turned_ref, shift_ref):
    def one(tile, carry):
        contract(d, values_ref, weights_ref, state_ref, gains_ref, squares_ref, tile)
        return carry

    def many(k, carry):
        for n in range(3):
            one(3 * k + n, carry)
        return carry

    lax.fori_loop(0, TILES // 3, many, 0)
    row = lax.broadcasted_iota(jnp.int32, (256, 128), 0)
    column = lax.broadcasted_iota(jnp.int32, (256, 128), 1)
    quarters = jnp.where(row // 16 % 4 == column % 4, 1.0, 0.0).astype(BF16)
    columns_ref[...] = jnp.dot(
        two_pieces(squares_ref[...].reshape(32 * TILES, 128)), quarters, preferred_element_type=F32
    )
    lane = lax.broadcasted_iota(jnp.int32, (32, 128), 1)
    tables = [jnp.zeros((32, 128), F32), jnp.zeros((32, 128), F32)]
    for tile in range(TILES):
        tables[tile // 32] = jnp.where(
            lane // 4 == tile % 32, columns_ref[32 * tile : 32 * tile + 32, :], tables[tile // 32]
        )
    for n in range(2):
        table = jnp.concatenate([tables[n], jnp.zeros((96, 128), F32)], axis=0)
        turned_ref[128 * n : 128 * n + 128, :] = jnp.transpose(table)
    rows = turned_ref[pl.ds(0, 40, stride=4), :]
    for q in range(1, 4):
        rows = rows + pltpu.roll(turned_ref[pl.ds(q, 40, stride=4), :], 32 * q, 1)
    begin = 8 * blocks_before(d)
    step = 128 * lax.broadcasted_iota(jnp.int32, (40, 128), 0) + lax.broadcasted_iota(jnp.int32, (40, 128), 1)
    shift_ref[0:32, :] = jnp.zeros((32, 128), F32)
    shift_ref[32:72, :] = pltpu.roll(jnp.where(step < 4096 - 16 * d, rows, 0.0), 16 * (d % 8), 1)
    back = 16 + 16 * (d % 8)
    later = pltpu.roll(jnp.where((step >= begin) & (step < begin + 16 * d + 16), rows, 0.0), 128 - back, 1)
    lane = lax.broadcasted_iota(jnp.int32, (32, 128), 1)
    near = shift_ref[pl.ds(32 - d // 8, 32), :]
    far = shift_ref[pl.ds(31 - d // 8, 32), :]
    return jnp.where(lane >= 16 * (d % 8), near, far) + jnp.where(lane < 128 - back, later[0:32], later[1:33])


def position():
    blk, mblk = lax.axis_index("blk"), lax.axis_index("mblk")
    return blk * 4 + mblk % 4, mblk // 4


def device_at(x, y):
    return (x // 4, y * 4 + x % 4)


def order_block(rank):
    return 4 * (rank % 32) + rank // 32


def greet(x, y):
    barrier = pltpu.get_barrier_semaphore()
    for step in range(1, 8):
        pl.semaphore_signal(barrier, inc=1, device_id=device_at((x + step) % 8, y), device_id_type=MESH)
    for step in range(1, 16):
        pl.semaphore_signal(barrier, inc=1, device_id=device_at(x, (y + step) % 16), device_id_type=MESH)
    return barrier


def send(source, target, send_sem, recv_sem, device):
    copy = pltpu.make_async_remote_copy(
        src_ref=source, dst_ref=target, send_sem=send_sem, recv_sem=recv_sem, device_id=device, device_id_type=MESH
    )
    copy.start()
    return copy


def drain(ref, sem):
    pltpu.make_async_copy(ref, ref, sem).wait()


def everything(
    pixels_hbm, ids_hbm, mask_hbm, model_hbm, logs_hbm, one_hbm, twist_hbm, two_hbm, low_hbm, high_hbm, spread_hbm, fold_hbm,
    pseudo_ref, misfit_ref,
    own_ref, ids_ref, mask_ref, model_ref, logs_ref, one_ref, twist_ref, two_ref, low_ref, high_ref, spread_ref, fold_ref,
    local_sem,
    rows_ref, mid_ref, joined_ref, again_ref, land_ref,
    coef_ref, gain_ref, wide_ref, broad_ref, gains_ref, state_ref, weights_ref, values_ref, squares_ref,
    columns_ref, turned_ref, shift_ref, part_ref, first_ref, second_ref, send_sem, recv_sem,
):
    x, y = position()
    d = order_block(x * 16 + y)
    barrier = greet(x, y)
    loads = [
        pltpu.make_async_copy(source, target, local_sem.at[n])
        for n, (source, target) in enumerate(
            (
                (low_hbm, low_ref), (high_hbm, high_ref), (spread_hbm, spread_ref), (one_hbm, one_ref),
                (twist_hbm, twist_ref), (two_hbm, two_ref), (fold_hbm, fold_ref), (pixels_hbm, own_ref),
                (ids_hbm, ids_ref), (mask_hbm, mask_ref), (model_hbm, model_ref), (logs_hbm, logs_ref),
            )
        )
    ]
    for copy in loads:
        copy.start()
    for copy in loads[0:3]:
        copy.wait()
    compact_tables(d, low_ref, high_ref, coef_ref, gain_ref)
    spread_coef(coef_ref, spread_ref, wide_ref)
    spread_gain(gain_ref, spread_ref, broad_ref, gains_ref)
    for copy in loads[3:]:
        copy.wait()
    fourier_body(y * 4 + x % 4, ids_ref, mask_ref, own_ref, one_ref, twist_ref, two_ref, logs_ref, rows_ref)
    pl.semaphore_wait(barrier, 22)
    for step in range(1, 8):
        to = (x + step) % 8
        send(rows_ref.at[to], mid_ref.at[x], send_sem.at[0], recv_sem.at[0], device_at(to, y))
    mid_ref[x] = rows_ref[x]
    zero = jnp.zeros((8, 128), F32)
    state = recur(d, wide_ref, values_ref, 0, CUT, (zero, zero, zero, zero))
    drain(mid_ref.at[pl.ds(0, 7)], recv_sem.at[0])
    for band in range(2):
        for n in range(4):
            at = 64 * band + 16 * n
            joined_ref[at : at + 16, :] = mid_ref[n, band] + mid_ref[4 + n, band]
    for to in range(16):
        again_ref[to] = joined_ref[pl.ds(to, 8, stride=16), :]
    for step in range(1, 16):
        to = (y + step) % 16
        send(again_ref.at[to], land_ref.at[y], send_sem.at[1], recv_sem.at[1], device_at(x, to))
    land_ref[y] = again_ref[y]
    recur(d, wide_ref, values_ref, CUT, 4 * TILES, state)
    drain(land_ref.at[pl.ds(0, 15)], recv_sem.at[1])
    prepare(land_ref, fold_ref, state_ref)
    widen_weights(state_ref, weights_ref)
    power = power_body(
        d, values_ref, weights_ref, state_ref, gains_ref, squares_ref, columns_ref, turned_ref, shift_ref
    )
    part_ref[...] = power
    first_ref[x] = power
    for step in range(1, 8):
        to = (x + step) % 8
        send(part_ref, first_ref.at[x], send_sem.at[2], recv_sem.at[2], device_at(to, y))
    drain(first_ref.at[pl.ds(0, 7)], recv_sem.at[2])
    second_ref[y] = jnp.sum(first_ref[...], axis=0)
    for step in range(1, 16):
        to = (y + step) % 16
        send(second_ref.at[y], second_ref.at[y], send_sem.at[3], recv_sem.at[3], device_at(x, to))
    drain(second_ref.at[pl.ds(0, 15)], recv_sem.at[3])
    pseudo = jnp.sum(second_ref[...], axis=0)
    pseudo_ref[...] = pseudo
    model = model_ref[...]
    rel_error = (pseudo - model) / model
    total = jnp.sum(rel_error * rel_error, keepdims=True)
    misfit_ref[...] = total * (1.0 / LMAX)
    drain(mid_ref.at[pl.ds(0, 7)], send_sem.at[0])
    drain(land_ref.at[pl.ds(0, 15)], send_sem.at[1])
    drain(first_ref.at[pl.ds(0, 7)], send_sem.at[2])
    drain(second_ref.at[pl.ds(0, 15)], send_sem.at[3])


VM = pl.BlockSpec(memory_space=pltpu.VMEM)
HB = pl.BlockSpec(memory_space=pl.ANY)


def on_device(pixels, block_ids, block_mask, model_cl):
    one, twist, two = dft_tables()
    low, high = degree_tables()
    spread = np.arange(128)[:, None] == 16 * (np.arange(1024) // 128) + np.arange(1024) % 16
    tables = (one, twist, two, low, high, spread.astype(jnp.bfloat16), fold_matrix())
    dma = pltpu.SemaphoreType.DMA
    pseudo_cl, misfit = pl.pallas_call(
        everything,
        out_shape=(jax.ShapeDtypeStruct((32, 128), F32), jax.ShapeDtypeStruct((1, 1), F32)),
        in_specs=[HB] * 12,
        out_specs=(VM, VM),
        scratch_shapes=[
            pltpu.VMEM((16, BLOCK_PIX), F32),
            pltpu.VMEM((1, 16), jnp.int32),
            pltpu.VMEM((1, 16), jnp.int32),
            pltpu.VMEM((32, 128), F32),
            pltpu.SMEM((CYCLES,), F32),
        ]
        + [pltpu.VMEM(table.shape, table.dtype) for table in tables]
        + [
            dma((12,)),
            pltpu.VMEM((8, 2, 16, 128), F32),
            pltpu.VMEM((8, 2, 16, 128), F32),
            pltpu.VMEM((128, 128), F32),
            pltpu.VMEM((16, 8, 128), F32),
            pltpu.VMEM((16, 8, 128), F32),
            pltpu.VMEM((ROWS, 128), F32),
            pltpu.VMEM((ROWS, 128), F32),
            pltpu.VMEM((8, ROWS, 128), F32),
            pltpu.VMEM((8 * ROWS, 128), F32),
            pltpu.VMEM((4 * TILES, 8, 128), F32),
            pltpu.VMEM((2, 10, 8, 128), F32),
            pltpu.VMEM((2, 2, 8, 2, 8, 128), F32),
            pltpu.VMEM((16 * TILES, 2, 64, 128), F32),
            pltpu.VMEM((4 * TILES, 8, 128), F32),
            pltpu.VMEM((32 * TILES, 128), F32),
            pltpu.VMEM((256, 128), F32),
            pltpu.VMEM((72, 128), F32),
            pltpu.VMEM((32, 128), F32),
            pltpu.VMEM((8, 32, 128), F32),
            pltpu.VMEM((16, 32, 128), F32),
            dma((4,)),
            dma((4,)),
        ],
        compiler_params=pltpu.CompilerParams(
            collective_id=0, has_side_effects=True, vmem_limit_bytes=60 * 1024 * 1024
        ),
    )(pixels, block_ids.reshape(1, 16), block_mask.reshape(1, 16), model_cl.reshape(32, 128), half_logs(), *tables)
    return pseudo_cl.reshape(LMAX), misfit.reshape(())


def solution(mesh):
    in_specs = (P(("blk", "mblk"), None), P(("blk", "mblk")), P(("blk", "mblk")), P())
    return jax.shard_map(on_device, mesh=mesh, in_specs=in_specs, out_specs=(P(), P()), check_vma=False)
```

```python
import functools
import math

import jax
import jax.numpy as jnp
import numpy as np
from jax import lax
from jax.experimental import pallas as pl
from jax.experimental.pallas import tpu as pltpu
from jax.sharding import PartitionSpec as P

NSIDE = 2048
CYCLE_PIX = 8192
LMAX = 4096
BLOCK_PIX = 1024
CYCLES = 256
DEVICES = 128
MESH = pl.DeviceIdType.MESH
HIGHEST = lax.Precision.HIGHEST
F32 = jnp.float32
BF16 = jnp.bfloat16
ROWS = 544
TILES = 33
CUT = 55


def dft_tables():
    k1 = np.arange(64)
    part, seg = np.meshgrid(np.arange(8), np.arange(8), indexing="ij")
    outer = (8 * seg + part).reshape(-1)
    angle = 2.0 * np.pi * ((k1[:, None] * outer[None, :]) % 64) / 64
    stage_one = np.concatenate([np.cos(angle), -np.sin(angle)], axis=0)
    inner = np.arange(128)
    twists = []
    stage_two = []
    upper = np.concatenate([np.arange(32), 63 - np.arange(32)])
    for cycle in range(2):
        shift = 0.5 if cycle == 0 else 0.0
        turn = 2.0 * np.pi * (k1[:, None] * (inner[None, :] + shift)) / CYCLE_PIX
        twists.append(np.stack([np.cos(turn), np.sin(turn)]))
        turn = 2.0 * np.pi * (upper[:, None] * inner[None, :] % 128) / 128 + (
            2.0 * np.pi * upper[:, None] * shift / 128
        )
        cos_two, sin_two = np.cos(turn), np.sin(turn)
        stage_two.append(
            np.concatenate(
                [
                    np.concatenate([cos_two, sin_two], axis=1),
                    np.concatenate([-sin_two, cos_two], axis=1),
                ],
                axis=0,
            )
        )
    return (
        stage_one.astype(np.float32),
        np.stack(twists).astype(np.float32),
        np.stack(stage_two).astype(np.float32),
    )


def half_logs():
    lat = (CYCLES // 2 - np.arange(CYCLES)) * (2.0 / (3.0 * NSIDE))
    return (0.5 * np.log1p(-lat * lat)).astype(np.float32)


def ratio_table():
    steps = np.arange(1, 4200, dtype=np.float64)
    prods = np.concatenate([[1.0], np.cumprod((2.0 * steps - 1.0) / (2.0 * steps))])
    j = np.arange(8384)
    even = 1.0 / (np.maximum(j, 1) * prods[j // 2])
    odd = prods[np.maximum(j - 1, 0) // 2]
    f = np.where(j % 2 == 0, even, odd)
    f[0] = 1.0
    return f


def degree_tables():
    f = ratio_table()
    step, lane = np.arange(128) // 16, np.arange(128) % 16
    diff = 8 * np.arange(528)[:, None] + (step - lane)[None, :]
    low = np.where(diff >= 0, f[np.maximum(diff, 0)], 0.0)
    high = f[8 * np.arange(1040)[:, None] + (step + lane)[None, :]]
    return low.astype(np.float32), high.astype(np.float32)


def fold_matrix():
    out = np.zeros((2, 2, 64, 128))
    for u in range(64):
        for c in range(2):
            south = 65 + u if c == 0 else 64 + u
            for odd in range(2):
                out[odd, c, u, 63 - u] += 1.0
                if south < 128:
                    out[odd, c, u, south] += -1.0 if odd else 1.0
    arrival = np.arange(128)
    y_source, x_source = arrival // 8, arrival % 8
    owner = (x_source // 4) * 64 + y_source * 4 + x_source % 4
    return out.reshape(256, 128)[:, owner].astype(np.float32)


EQUATOR_ROW = 4


def fourier_body(pair, ids_ref, mask_ref, own_ref, one_ref, twist_ref, two_ref, logs_ref, out_ref):
    row = lax.broadcasted_iota(jnp.int32, (32, 16), 0)
    slot = (pair + 64 * (row // 16)) * 16 + row % 16
    pick = jnp.where(ids_ref[...] == slot, mask_ref[...], 0).astype(F32)
    rows = jnp.dot(pick, own_ref[...], precision=HIGHEST, preferred_element_type=F32)
    folded = jnp.concatenate(
        [
            jnp.concatenate([rows[8 * n : 8 * n + 8, 128 * p : 128 * p + 128] for p in range(8)], axis=0)
            for n in range(4)
        ],
        axis=1,
    )
    first = jnp.dot(one_ref[...], folded, precision=HIGHEST, preferred_element_type=F32)
    k1 = lax.broadcasted_iota(jnp.int32, (64, 64), 1)
    upper = lax.broadcasted_iota(jnp.int32, (64, 64), 0)
    orders = (k1 + 64 * jnp.where(upper < 32, upper, 95 - upper)).astype(F32)
    outs = [[None, None], [None, None]]
    for c in range(2):
        cos, sin = twist_ref[c, 0], twist_ref[c, 1]
        turned = []
        for band in range(2):
            lanes = slice(128 * (2 * band + c), 128 * (2 * band + c) + 128)
            re, im = first[0:64, lanes], first[64:128, lanes]
            turned.append(jnp.concatenate([re * cos + im * sin, im * cos - re * sin], axis=1))
        spec = lax.dot_general(
            two_ref[c],
            jnp.concatenate(turned, axis=0),
            (((1,), (1,)), ((), ())),
            precision=HIGHEST,
            preferred_element_type=F32,
        )
        for band in range(2):
            seed = jnp.exp(orders * logs_ref[2 * (pair + 64 * band) + c])
            lanes = slice(64 * band, 64 * band + 64)
            outs[band][c] = (spec[0:64, lanes] * seed, spec[64:128, lanes] * seed)
    for band in range(2):
        for j in range(4):
            pieces = []
            for ri in range(2):
                for half in range(2):
                    jj = j if half == 0 else 3 - j
                    for c in range(2):
                        pieces.append(outs[band][c][ri][32 * half : 32 * half + 32, 16 * jj : 16 * jj + 16])
            joined = jnp.concatenate(pieces, axis=1)
            for n in range(2):
                out_ref[2 * j + n, band] = joined[16 * n : 16 * n + 16]


def two_pieces(value):
    high = value.astype(BF16)
    return jnp.concatenate([high, (value - high.astype(F32)).astype(BF16)], axis=1)


def pieces_of(value):
    high = value.astype(BF16)
    rest = value - high.astype(F32)
    middle = rest.astype(BF16)
    return high, middle, (rest - middle.astype(F32)).astype(BF16)


def blocks_before(d):
    return 512 - 16 * (d // 8)


def compact_tables(d, low_ref, high_ref, coef_ref, gain_ref):
    row = lax.broadcasted_iota(jnp.int32, (8, 128), 0)
    lane = lax.broadcasted_iota(jnp.int32, (8, 128), 1)
    order = lane % 16
    offset = 8 * row + lane // 16
    coef_ref[...] = jnp.zeros((ROWS, 128), F32)
    gain_ref[...] = jnp.zeros((ROWS, 128), F32)
    for half in range(2):
        first = first_order(d, half)
        start = 0 if half == 0 else blocks_before(d)

        def one(k, carry):
            low = low_ref[pl.ds(pl.multiple_of(8 * k, 8), 8), :]
            high = high_ref[pl.ds(first // 4 + 8 * k, 8), :]
            both = low * high
            t = offset + 64 * k
            degree = t + first
            down = t - order
            up = (degree + first + order).astype(F32)
            weight = jnp.where(first + order == 0, 1.0, 2.0)
            denom = jnp.maximum(down.astype(F32), 1.0) * jnp.maximum(up, 1.0) * both
            at = pl.ds(start + 8 * k, 8)
            coef_ref[at, :] = both * (2 * degree - 1).astype(F32)
            gain_ref[at, :] = jnp.where(down >= 0, weight / jnp.where(down >= 0, denom, 1.0), 0.0)
            return carry

        lax.fori_loop(0, (4096 - first + 63) // 64, one, 0)


def spread_coef(coef_ref, spread_ref, wide_ref):
    spread = spread_ref[...]
    for chunk in range(4):
        at = pl.ds(ROWS // 4 * chunk, ROWS // 4)
        total = None
        for piece in pieces_of(coef_ref[at, :]):
            part = jnp.dot(piece, spread, preferred_element_type=F32)
            total = part if total is None else total + part
        for step in range(8):
            wide_ref[step, at, :] = total[:, 128 * step : 128 * step + 128]


def spread_gain(gain_ref, spread_ref, wide_ref, gains_ref):
    spread = jnp.concatenate([spread_ref[...]] * 2, axis=0)
    for chunk in range(4):
        start = ROWS // 4 * chunk
        total = jnp.dot(two_pieces(gain_ref[pl.ds(start, ROWS // 4), :]), spread, preferred_element_type=F32)
        for step in range(8):
            wide_ref[pl.ds(8 * start + step, ROWS // 4, stride=8), :] = total[:, 128 * step : 128 * step + 128]
    quarter = lax.broadcasted_iota(jnp.int32, (8, 128), 1) // 16 % 4

    def one(tile, carry):
        for n in range(4):
            packed = None
            for q in range(4):
                rows = wide_ref[pl.ds(pl.multiple_of(128 * tile + 32 * q + 8 * n, 8), 8), :]
                packed = rows if packed is None else jnp.where(quarter == q, rows, packed)
            gains_ref[4 * tile + n] = packed
        return carry

    def many(k, carry):
        for n in range(3):
            one(3 * k + n, carry)
        return carry

    lax.fori_loop(0, TILES // 3, many, 0)


def prepare(got_ref, fold_ref, state_ref):
    row = lax.broadcasted_iota(jnp.int32, (64, 128), 0)
    lane = lax.broadcasted_iota(jnp.int32, (64, 128), 1)
    got = got_ref[...].reshape(128, 128)
    folded = jnp.dot(fold_ref[...], got, precision=HIGHEST, preferred_element_type=F32)
    is_c0 = (lane % 32) < 16
    even = jnp.where(is_c0, folded[0:64], folded[64:128])
    odd = jnp.where(is_c0, folded[128:192], folded[192:256])
    same = (lane % 2) == 0
    by_parity = (jnp.where(same, even, odd), jnp.where(same, odd, even))
    group = lax.broadcasted_iota(jnp.int32, (8, 128), 1) // 32
    for half in range(2):
        for p in range(2):
            for ri in range(2):
                source = 2 * ri + half
                for v in range(2):
                    total = None
                    for h in range(4):
                        piece = by_parity[p][32 * v + 8 * h : 32 * v + 8 * h + 8]
                        moved = pltpu.roll(piece, (32 * (h - source)) % 128, 1)
                        total = moved if total is None else jnp.where(group == h, moved, total)
                    state_ref[half, 4 * p + 2 * ri + v] = total
    step = lax.broadcasted_iota(jnp.int32, (8, 128), 0)
    lane8 = lax.broadcasted_iota(jnp.int32, (8, 128), 1)
    turn = (step - lane8 % 16) & 3
    sign = jnp.where(turn == 0, 1.0, jnp.where(turn == 2, -1.0, 0.0))
    line = jnp.broadcast_to(got[EQUATOR_ROW : EQUATOR_ROW + 1, :], (8, 128))
    for half in range(2):
        for ri in range(2):
            source = 2 * ri + half
            base = jnp.where(lane8 // 16 == 2 * source, line, 0.0)
            base = pltpu.roll(base, (128 - 32 * source) % 128, 1)
            state_ref[half, 8 + ri] = base * sign


def first_order(d, half):
    return 16 * d if half == 0 else 4080 - 16 * d


def first_order(d, half):
    return 16 * d if half == 0 else 4080 - 16 * d


def latitudes():
    row = lax.broadcasted_iota(jnp.int32, (8, 128), 0)
    lane = lax.broadcasted_iota(jnp.int32, (8, 128), 1)
    lats = []
    for v in range(2):
        u = 32 * v + 8 * (lane // 32) + row
        q = 2 * u + jnp.where((lane % 32) < 16, 2, 1)
        lats.append(q.astype(F32) * (2.0 / (3.0 * NSIDE)))
    return lats


def value_of(order, fresh, step):
    return jnp.where(order == step, fresh, 0.0)


def recur(d, coef_ref, values_ref, low, top, state):
    order = lax.broadcasted_iota(jnp.int32, (8, 128), 1) % 16
    lats = latitudes()
    restart = blocks_before(d) // 4

    def quad(n, state):
        fresh = jnp.where((n == 0) | (n == restart), 1.0, 0.0)
        a0, a1, b0, b1 = [value * (1.0 - fresh) for value in state]
        for step in range(0, 32, 2):
            block = 4 * n + step // 8
            now, later = [
                jnp.broadcast_to(coef_ref[(step + k) % 8, pl.ds(block, 1), :], (8, 128)) for k in range(2)
            ]
            ones = [value_of(order, fresh, step + k) for k in range(2)] if step < 16 else None
            fresh_pair = []
            for v, (one_back, two_back) in enumerate(((a0, b0), (a1, b1))):
                c0, c1 = now * lats[v], later * lats[v]
                if ones is not None:
                    two_back = two_back - ones[0]
                rest = c1 * two_back
                if ones is not None:
                    rest = rest - ones[1]
                first = c0 * one_back - two_back
                second = (c1 * c0 - 1.0) * one_back - rest
                values_ref[block, v, pl.ds(step % 8, 8, stride=8), :] = first
                values_ref[block, v, pl.ds(step % 8 + 1, 8, stride=8), :] = second
                fresh_pair.append((second, first))
            (a0, b0), (a1, b1) = fresh_pair
        return (a0, a1, b0, b1)

    return lax.fori_loop(low, top, quad, state)


def widen_weights(state_ref, weights_ref):
    even_row = (lax.broadcasted_iota(jnp.int32, (8, 128), 0) & 1) == 0
    for half in range(2):
        for v in range(2):
            for ri in range(2):
                even, odd = state_ref[half, 2 * ri + v], state_ref[half, 4 + 2 * ri + v]
                for s in range(8):
                    weights_ref[half, v, s, ri] = jnp.where(
                        even_row,
                        jnp.broadcast_to(even[s : s + 1], (8, 128)),
                        jnp.broadcast_to(odd[s : s + 1], (8, 128)),
                    )


def contract(d, values_ref, weights_ref, state_ref, gains_ref, squares_ref, tile):
    lane = lax.broadcasted_iota(jnp.int32, (8, 128), 1)
    masks = {shift: (lane & shift) == 0 for shift in (16, 32, 64)}

    def merge(shift, first, second):
        mask = masks[shift]
        return jnp.where(mask, first, second) + pltpu.roll(jnp.where(mask, second, first), 128 - shift, 1)

    half = jnp.where(16 * tile >= blocks_before(d), 1, 0)
    for n in range(4):
        blocks = [16 * tile + n + 4 * q for q in range(4)]
        sums = [[state_ref[half, 8 + ri]] * 4 for ri in range(2)]
        for v in range(2):
            for s in range(8):
                weights = [weights_ref[half, v, s, ri] for ri in range(2)]
                for q in range(4):
                    value = values_ref[blocks[q], v, 8 * s : 8 * s + 8, :]
                    for ri in range(2):
                        sums[ri][q] = sums[ri][q] + value * weights[ri]
        parts = [
            merge(32, merge(16, sums[ri][0], sums[ri][1]), merge(16, sums[ri][2], sums[ri][3])) for ri in range(2)
        ]
        packed = merge(64, parts[0], parts[1])
        squares_ref[4 * tile + n] = packed * packed * gains_ref[4 * tile + n]


def power_body(d, values_ref, weights_ref, state_ref, gains_ref, squares_ref, columns_ref, turned_ref, shift_ref):
    def one(tile, carry):
        contract(d, values_ref, weights_ref, state_ref, gains_ref, squares_ref, tile)
        return carry

    def many(k, carry):
        for n in range(4):
            one(4 * k + n, carry)
        return carry

    lax.fori_loop(0, TILES // 4, many, 0)
    one(TILES - 1, 0)
    row = lax.broadcasted_iota(jnp.int32, (256, 128), 0)
    column = lax.broadcasted_iota(jnp.int32, (256, 128), 1)
    quarters = jnp.where(row // 16 % 4 == column % 4, 1.0, 0.0).astype(BF16)
    columns_ref[...] = jnp.dot(
        two_pieces(squares_ref[...].reshape(32 * TILES, 128)), quarters, preferred_element_type=F32
    )
    lane = lax.broadcasted_iota(jnp.int32, (32, 128), 1)
    tables = [jnp.zeros((32, 128), F32), jnp.zeros((32, 128), F32)]
    for tile in range(TILES):
        tables[tile // 32] = jnp.where(
            lane // 4 == tile % 32, columns_ref[32 * tile : 32 * tile + 32, :], tables[tile // 32]
        )
    for n in range(2):
        table = jnp.concatenate([tables[n], jnp.zeros((96, 128), F32)], axis=0)
        turned_ref[128 * n : 128 * n + 128, :] = jnp.transpose(table)
    rows = turned_ref[pl.ds(0, 40, stride=4), :]
    for q in range(1, 4):
        rows = rows + pltpu.roll(turned_ref[pl.ds(q, 40, stride=4), :], 32 * q, 1)
    begin = 8 * blocks_before(d)
    step = 128 * lax.broadcasted_iota(jnp.int32, (40, 128), 0) + lax.broadcasted_iota(jnp.int32, (40, 128), 1)
    shift_ref[0:32, :] = jnp.zeros((32, 128), F32)
    shift_ref[32:72, :] = pltpu.roll(jnp.where(step < 4096 - 16 * d, rows, 0.0), 16 * (d % 8), 1)
    back = 16 + 16 * (d % 8)
    later = pltpu.roll(jnp.where((step >= begin) & (step < begin + 16 * d + 16), rows, 0.0), 128 - back, 1)
    lane = lax.broadcasted_iota(jnp.int32, (32, 128), 1)
    near = shift_ref[pl.ds(32 - d // 8, 32), :]
    far = shift_ref[pl.ds(31 - d // 8, 32), :]
    return jnp.where(lane >= 16 * (d % 8), near, far) + jnp.where(lane < 128 - back, later[0:32], later[1:33])


def position():
    blk, mblk = lax.axis_index("blk"), lax.axis_index("mblk")
    return blk * 4 + mblk % 4, mblk // 4


def device_at(x, y):
    return (x // 4, y * 4 + x % 4)


def order_block(rank):
    return 4 * (rank % 32) + rank // 32


def greet(x, y):
    barrier = pltpu.get_barrier_semaphore()
    for step in range(1, 8):
        pl.semaphore_signal(barrier, inc=1, device_id=device_at((x + step) % 8, y), device_id_type=MESH)
    for step in range(1, 16):
        pl.semaphore_signal(barrier, inc=1, device_id=device_at(x, (y + step) % 16), device_id_type=MESH)
    return barrier


def send(source, target, send_sem, recv_sem, device):
    copy = pltpu.make_async_remote_copy(
        src_ref=source, dst_ref=target, send_sem=send_sem, recv_sem=recv_sem, device_id=device, device_id_type=MESH
    )
    copy.start()
    return copy


def drain(ref, sem):
    pltpu.make_async_copy(ref, ref, sem).wait()


def everything(
    pixels_hbm, ids_hbm, mask_hbm, model_hbm, logs_hbm, one_hbm, twist_hbm, two_hbm, low_hbm, high_hbm, spread_hbm, fold_hbm,
    pseudo_ref, misfit_ref,
    own_ref, ids_ref, mask_ref, model_ref, logs_ref, one_ref, twist_ref, two_ref, low_ref, high_ref, spread_ref, fold_ref,
    local_sem,
    rows_ref, mid_ref, joined_ref, again_ref, land_ref,
    coef_ref, gain_ref, wide_ref, broad_ref, gains_ref, state_ref, weights_ref, values_ref, squares_ref,
    columns_ref, turned_ref, shift_ref, part_ref, first_ref, second_ref, send_sem, recv_sem,
):
    x, y = position()
    d = order_block(x * 16 + y)
    barrier = greet(x, y)
    loads = [
        pltpu.make_async_copy(source, target, local_sem.at[n])
        for n, (source, target) in enumerate(
            (
                (low_hbm, low_ref), (high_hbm, high_ref), (spread_hbm, spread_ref), (one_hbm, one_ref),
                (twist_hbm, twist_ref), (two_hbm, two_ref), (fold_hbm, fold_ref), (pixels_hbm, own_ref),
                (ids_hbm, ids_ref), (mask_hbm, mask_ref), (model_hbm, model_ref), (logs_hbm, logs_ref),
            )
        )
    ]
    for copy in loads:
        copy.start()
    for copy in loads[0:3]:
        copy.wait()
    compact_tables(d, low_ref, high_ref, coef_ref, gain_ref)
    spread_coef(coef_ref, spread_ref, wide_ref)
    spread_gain(gain_ref, spread_ref, broad_ref, gains_ref)
    for copy in loads[3:]:
        copy.wait()
    fourier_body(y * 4 + x % 4, ids_ref, mask_ref, own_ref, one_ref, twist_ref, two_ref, logs_ref, rows_ref)
    pl.semaphore_wait(barrier, 22)
    for step in range(1, 8):
        to = (x + step) % 8
        send(rows_ref.at[to], mid_ref.at[x], send_sem.at[0], recv_sem.at[0], device_at(to, y))
    mid_ref[x] = rows_ref[x]
    zero = jnp.zeros((8, 128), F32)
    state = recur(d, wide_ref, values_ref, 0, CUT, (zero, zero, zero, zero))
    drain(mid_ref.at[pl.ds(0, 7)], recv_sem.at[0])
    for band in range(2):
        for n in range(4):
            at = 64 * band + 16 * n
            joined_ref[at : at + 16, :] = mid_ref[n, band] + mid_ref[4 + n, band]
    for to in range(16):
        again_ref[to] = joined_ref[pl.ds(to, 8, stride=16), :]
    for step in range(1, 16):
        to = (y + step) % 16
        send(again_ref.at[to], land_ref.at[y], send_sem.at[1], recv_sem.at[1], device_at(x, to))
    land_ref[y] = again_ref[y]
    recur(d, wide_ref, values_ref, CUT, 4 * TILES, state)
    drain(land_ref.at[pl.ds(0, 15)], recv_sem.at[1])
    prepare(land_ref, fold_ref, state_ref)
    widen_weights(state_ref, weights_ref)
    power = power_body(
        d, values_ref, weights_ref, state_ref, gains_ref, squares_ref, columns_ref, turned_ref, shift_ref
    )
    part_ref[...] = power
    first_ref[x] = power
    for step in range(1, 8):
        to = (x + step) % 8
        send(part_ref, first_ref.at[x], send_sem.at[2], recv_sem.at[2], device_at(to, y))
    drain(first_ref.at[pl.ds(0, 7)], recv_sem.at[2])
    second_ref[y] = jnp.sum(first_ref[...], axis=0)
    for step in range(1, 16):
        to = (y + step) % 16
        send(second_ref.at[y], second_ref.at[y], send_sem.at[3], recv_sem.at[3], device_at(x, to))
    drain(second_ref.at[pl.ds(0, 15)], recv_sem.at[3])
    pseudo = jnp.sum(second_ref[...], axis=0)
    pseudo_ref[...] = pseudo
    model = model_ref[...]
    rel_error = (pseudo * (1.0 / (CYCLES * CYCLE_PIX)) - model) / model
    total = jnp.sum(rel_error * rel_error, keepdims=True)
    misfit_ref[...] = total * (1.0 / LMAX)
    drain(mid_ref.at[pl.ds(0, 7)], send_sem.at[0])
    drain(land_ref.at[pl.ds(0, 15)], send_sem.at[1])
    drain(first_ref.at[pl.ds(0, 7)], send_sem.at[2])
    drain(second_ref.at[pl.ds(0, 15)], send_sem.at[3])


VM = pl.BlockSpec(memory_space=pltpu.VMEM)
HB = pl.BlockSpec(memory_space=pl.ANY)


def on_device(pixels, block_ids, block_mask, model_cl):
    one, twist, two = dft_tables()
    low, high = degree_tables()
    spread = np.arange(128)[:, None] == 16 * (np.arange(1024) // 128) + np.arange(1024) % 16
    tables = (one, twist, two, low, high, spread.astype(jnp.bfloat16), fold_matrix())
    dma = pltpu.SemaphoreType.DMA
    pseudo_cl, misfit = pl.pallas_call(
        everything,
        out_shape=(jax.ShapeDtypeStruct((32, 128), F32), jax.ShapeDtypeStruct((1, 1), F32)),
        in_specs=[HB] * 12,
        out_specs=(VM, VM),
        scratch_shapes=[
            pltpu.VMEM((16, BLOCK_PIX), F32),
            pltpu.VMEM((1, 16), jnp.int32),
            pltpu.VMEM((1, 16), jnp.int32),
            pltpu.VMEM((32, 128), F32),
            pltpu.SMEM((CYCLES,), F32),
        ]
        + [pltpu.VMEM(table.shape, table.dtype) for table in tables]
        + [
            dma((12,)),
            pltpu.VMEM((8, 2, 16, 128), F32),
            pltpu.VMEM((8, 2, 16, 128), F32),
            pltpu.VMEM((128, 128), F32),
            pltpu.VMEM((16, 8, 128), F32),
            pltpu.VMEM((16, 8, 128), F32),
            pltpu.VMEM((ROWS, 128), F32),
            pltpu.VMEM((ROWS, 128), F32),
            pltpu.VMEM((8, ROWS, 128), F32),
            pltpu.VMEM((8 * ROWS, 128), F32),
            pltpu.VMEM((4 * TILES, 8, 128), F32),
            pltpu.VMEM((2, 10, 8, 128), F32),
            pltpu.VMEM((2, 2, 8, 2, 8, 128), F32),
            pltpu.VMEM((16 * TILES, 2, 64, 128), F32),
            pltpu.VMEM((4 * TILES, 8, 128), F32),
            pltpu.VMEM((32 * TILES, 128), F32),
            pltpu.VMEM((256, 128), F32),
            pltpu.VMEM((72, 128), F32),
            pltpu.VMEM((32, 128), F32),
            pltpu.VMEM((8, 32, 128), F32),
            pltpu.VMEM((16, 32, 128), F32),
            dma((4,)),
            dma((4,)),
        ],
        compiler_params=pltpu.CompilerParams(
            collective_id=0, has_side_effects=True, vmem_limit_bytes=60 * 1024 * 1024
        ),
    )(pixels, block_ids.reshape(1, 16), block_mask.reshape(1, 16), model_cl.reshape(32, 128), half_logs(), *tables)
    return pseudo_cl.reshape(LMAX) * (1.0 / (CYCLES * CYCLE_PIX)), misfit.reshape(())


def solution(mesh):
    in_specs = (P(("blk", "mblk"), None), P(("blk", "mblk")), P(("blk", "mblk")), P())
    return jax.shard_map(on_device, mesh=mesh, in_specs=in_specs, out_specs=(P(), P()), check_vma=False)
```
